512 devices in a mesh: context: 64 (over x_hi, z, core), tensor: 8 (over y, x_lo).
Axes of the slice: x: 4 (x_hi: 2, x_lo: 2; x = x_hi * 2 + x_lo), y: 4, z: 16, core: 2. Of those that a mesh axis runs over, the one named last changes fastest.
Arguments:
- query: bfloat16 [2, 8192, 8192], P(None, 'context', 'tensor'), may hold values from -6 to 6
- key: bfloat16 [2, 8192, 8192], P(None, 'context', 'tensor'), may hold values from -6 to 6
- value: bfloat16 [2, 8192, 8192], P(None, 'context', 'tensor'), may hold values from -6 to 6
- grad_out: bfloat16 [2, 8192, 8192], P(None, 'context', 'tensor'), may hold values from -6 to 6
- residue: float32 [16, 256], replicated, may hold values from -0.06 to 0.06
- rate: float32 [16, 256], replicated, may hold values from 0 to 1, as said below
Outputs:
- mixed: bfloat16 [2, 8192, 8192], P(None, 'context', 'tensor')
- grad_query: bfloat16 [2, 8192, 8192], P(None, 'context', 'tensor')
- grad_key: bfloat16 [2, 8192, 8192], P(None, 'context', 'tensor')
- grad_value: bfloat16 [2, 8192, 8192], P(None, 'context', 'tensor')
- grad_residue: float32 [16, 256], replicated
The draws below stay inside these ranges and needn't reach their ends.
Inputs may be any that keep to these rules, and one draw needn't show every extreme that they name: Every rate lies between 0.25 / 8192 and 1/24.
All inputs are finite; a program needn't handle non-finite values.
Results may differ from the reference program's by a relative error of at most 0.0055.
Values sent between devices are 32-bit elements; how exact they have to be, the bound alone decides.
No kernel may reach another device: no remote copies, remote signals or barrier semaphores. Data moves between devices by JAX's collectives and lax.ppermute only.
A program may use at most 128 MiB of HBM per device.

```python
import jax
import jax.numpy as jnp
from jax import lax

C = 8192
FILTERS = 256
MODES = 16
SEQS = 2
TOK_DEV = 128
LEN = 8192


def draw_rate(key, part):
    pick_key, slow_key, fast_key = jax.random.split(jax.random.fold_in(key, 17), 3)
    table_shape = (MODES, FILTERS)
    slow_rates = jnp.exp(jax.random.uniform(slow_key, table_shape, jnp.float32, jnp.log(0.25 / LEN), jnp.log(2.0 / LEN)))
    fast_rates = jnp.exp(jax.random.uniform(fast_key, table_shape, jnp.float32, jnp.log(2.0 / LEN), jnp.log(1.0 / 24.0)))
    keep_mask = jax.random.uniform(pick_key, table_shape) < 0.5
    return jnp.where(keep_mask, slow_rates, fast_rates).astype(jnp.float32)


def steps_of(key, shape, shards, low, top_value):
    def one(dim, blocks):
        heights = jax.random.uniform(jax.random.fold_in(jax.random.fold_in(key, 6), dim), (blocks,), jnp.float32, low / len(shards), top_value / len(shards))
        return jnp.repeat(jnp.exp(heights), shape[dim] // blocks).reshape((-1,) + (1,) * (len(shape) - dim - 1))

    factor_of = one(*shards[0])
    for cut in shards[1:]:
        factor_of = factor_of * one(*cut)
    return factor_of


def noise(key, extent, spread, most, shards=(), kind=jnp.bfloat16):
    array = jax.random.normal(key, extent, jnp.float32) * spread
    if len(shards) > 0:
        array = steps_of(key, extent, shards, -0.22, 0.18) * array
    return jnp.clip(array, min=-most, max=most).astype(kind)


def setup_inputs(seed: int = 0) -> dict:
    streams_of = jax.random.split(jax.random.key(seed), 7)
    query = noise(streams_of[0], (SEQS, LEN, C), 1.0, 6.0, ((1, 64), (2, 8)))
    key = noise(streams_of[1], (SEQS, LEN, C), 1.0, 6.0, ((1, 64), (2, 8)))
    value = noise(streams_of[2], (SEQS, LEN, C), 1.0, 6.0, ((1, 64), (2, 8)))
    grad_out = noise(streams_of[3], (SEQS, LEN, C), 1.0, 6.0, ((1, 64), (2, 8)))
    residue = noise(streams_of[4], (MODES, FILTERS), 0.01, 0.06, (), jnp.float32)
    rate = draw_rate(jax.random.fold_in(streams_of[6], 71), 0)
    return {"query": query, "key": key, "value": value, "grad_out": grad_out, "residue": residue, "rate": rate}


highest = lax.Precision.HIGHEST

def convolve(inputs, residue, rate):
    seq_count, length, channels = inputs.shape
    repeat = channels // FILTERS
    block_count = length // TOK_DEV
    blocked = inputs.reshape(seq_count, block_count, TOK_DEV, repeat, FILTERS).transpose(1, 0, 2, 3, 4)
    position = jnp.arange(TOK_DEV, dtype=jnp.float32)
    distance = position[:, None] - position[None, :]
    lower_mask = distance >= 0.0
    clipped = jnp.where(lower_mask, distance, 0.0)
    toeplitz = jnp.zeros((FILTERS, TOK_DEV, TOK_DEV), jnp.float32)
    for mode_index in range(MODES):
        toeplitz = toeplitz + residue[mode_index][:, None, None] * jnp.exp(-rate[mode_index][:, None, None] * clipped[None])
    toeplitz = jnp.where(lower_mask[None], toeplitz, 0.0)
    into_rows = residue[:, :, None] * jnp.exp(-rate[:, :, None] * (position + 1.0))
    out_rows = jnp.exp(-rate[:, :, None] * (TOK_DEV - 1.0 - position))
    block_decay = jnp.exp(-rate * TOK_DEV)

    def advance(state, piece):
        nearby = jnp.einsum('fab,sbrf->sarf', toeplitz, piece, precision=highest)
        carried = jnp.einsum('nfa,nsrf->sarf', into_rows, state, precision=highest)
        state = block_decay[:, None, None, :] * state + jnp.einsum('nfb,sbrf->nsrf', out_rows, piece, precision=highest)
        return (state, nearby + carried)
    initial = jnp.zeros((MODES, seq_count, repeat, FILTERS), jnp.float32)
    _, outputs = lax.scan(advance, initial, blocked)
    return outputs.transpose(1, 0, 2, 3, 4).reshape(seq_count, length, channels)

def forward(query, key, value, residue, rate):
    inputs = key.astype(jnp.float32) * value.astype(jnp.float32)
    mixed_z = convolve(inputs, residue, rate)
    return (query.astype(jnp.float32) * mixed_z).astype(jnp.bfloat16)

def reference(query, key, value, grad_out, residue, rate):

    def with_rate(query_in, key_in, value_in, residue_in):
        return forward(query_in, key_in, value_in, residue_in, rate)
    mixed, pullback = jax.vjp(with_rate, query, key, value, residue)
    grad_query, grad_key, grad_value, grad_residue = pullback(grad_out)
    return (mixed, grad_query, grad_key, grad_value, grad_residue / float(SEQS * LEN))
```

```python
import functools

import jax
import jax.numpy as jnp
from jax import lax
from jax.experimental import pallas as pl
from jax.experimental.pallas import tpu as pltpu
from jax.sharding import Mesh, PartitionSpec as P

F32 = jnp.float32
LANES = 128
MODES = 16
ROWS = 9


def spread(row):
    return jnp.broadcast_to(row, (8, LANES))


def bottom():
    return lax.broadcasted_iota(jnp.int32, (8, LANES), 0) >= 4


def swap_halves(tile):
    return pltpu.roll(tile, 4, 0)


def lanes_of(half):
    return pl.ds(half * LANES, LANES)


def local_kernel(core, query, key, value, grad, residue, rate, near, back, keep, send, within, work_u, work_g):
    length = query.shape[1]
    repeat = query.shape[2] // (2 * LANES)
    first = core[0] == 0
    for half in range(2):
        for seq in range(2):
            for rep in range(repeat):
                cut = pl.ds(rep * 2 * LANES + half * LANES, LANES)
                rows = pl.ds(seq * repeat + rep, length, stride=8)
                work_u[rows, :] = key[seq, :, cut].astype(F32) * value[seq, :, cut].astype(F32)
                work_g[rows, :] = grad[seq, :, cut].astype(F32) * query[seq, :, cut].astype(F32)
        for group in range(0, MODES, 8):
            modes = range(group, group + 8)
            decay = [spread(jnp.exp(-rate[n : n + 1, lanes_of(half)])) for n in modes]
            weight = [spread(residue[n : n + 1, lanes_of(half)]) for n in modes]

            def step(i, carry, decay=decay, weight=weight, group=group, half=half):
                ups, downs, sums = (list(c) for c in carry)
                ahead = pl.ds(pl.multiple_of(i * 8, 8), 8)
                behind = pl.ds(pl.multiple_of((length - 1 - i) * 8, 8), 8)
                u, g, gr = work_u[ahead, :], work_g[ahead, :], work_g[behind, :]
                parts, parts_back = [], []
                for m in range(8):
                    ups[m] = decay[m] * ups[m] + u
                    downs[m] = decay[m] * downs[m] + gr
                    sums[m] = sums[m] + g * ups[m]
                    parts.append(weight[m] * ups[m])
                    parts_back.append(weight[m] * downs[m])
                z, dz = tree(parts), tree(parts_back)
                if group:
                    z, dz = z + near[half, ahead, :], dz + back[half, behind, :]
                near[half, ahead, :] = z
                back[half, behind, :] = dz
                return tuple(ups), tuple(downs), tuple(sums)

            zero = tuple(jnp.zeros((8, LANES), F32) for _ in range(8))
            ups, downs, sums = lax.fori_loop(0, length, step, (zero, zero, zero), unroll=2)
            low = bottom()
            for m in range(8):
                top_half = jnp.where(low, swap_halves(downs[m]), ups[m])
                end_half = jnp.where(low, downs[m], swap_halves(ups[m]))
                piece = half * MODES + group + m
                keep[piece] = jnp.where(first, top_half, end_half)
                send[piece] = jnp.where(first, end_half, top_half)
                within[piece : piece + 1, :] = jnp.sum(sums[m], axis=0, keepdims=True)


def tree(parts):
    while len(parts) > 1:
        parts = [parts[i] + parts[i + 1] for i in range(0, len(parts), 2)]
    return parts[0]


def order(first, own, other):
    return jnp.where(first, own, other), jnp.where(first, other, own)


def pair_kernel(core, own, other, within, rate, out, *, block):
    first = core[0] == 0
    low = bottom()
    for half in range(2):
        for n in range(MODES):
            piece = half * MODES + n
            pace = rate[n : n + 1, lanes_of(half)]
            decay = spread(jnp.exp(-pace * float(block)))
            left, right = order(first, own[piece], other[piece])
            joined = jnp.where(low, left + decay * right, decay * left + right)
            cross = jnp.where(low, 0.0, left * swap_halves(right))
            total = jnp.exp(-pace) * jnp.sum(cross, axis=0, keepdims=True)
            for row in range(8):
                out[piece * ROWS + row] = joined[row : row + 1, :]
            out[piece * ROWS + 8] = within[piece : piece + 1, :] + total


def scan_kernel(pieces, pace, out, *, block):
    count = pieces.shape[0] // ROWS
    decay = jnp.exp(-pace[...] * float(block))
    decay4 = jnp.broadcast_to(decay, (4, LANES))

    def load(index, base):
        return jnp.concatenate([pieces[index * ROWS + base + j] for j in range(4)], axis=0)

    ahead = jnp.zeros((4, LANES), F32)
    cross = jnp.zeros((4, LANES), F32)
    local = jnp.zeros((1, LANES), F32)
    for index in range(count):
        for j in range(4):
            out[index * ROWS + j] = ahead[j : j + 1, :]
        cross = cross + ahead * load(index, 4)
        local = local + pieces[index * ROWS + 8]
        ahead = decay4 * ahead + load(index, 0)
    behind = jnp.zeros((4, LANES), F32)
    for index in reversed(range(count)):
        for j in range(4):
            out[index * ROWS + 4 + j] = behind[j : j + 1, :]
        behind = decay4 * behind + load(index, 4)
    total = local + jnp.exp(-pace[...]) * jnp.sum(cross, axis=0, keepdims=True)
    for index in range(count):
        out[index * ROWS + 8] = total


def split_kernel(core, pieces, own, other, rate, keep, send, total, *, block):
    first = core[0] == 0
    low = bottom()
    for half in range(2):
        for n in range(MODES):
            piece = half * MODES + n
            pace = rate[n : n + 1, lanes_of(half)]
            decay = spread(jnp.exp(-pace * float(block)))
            left, right = order(first, own[piece], other[piece])
            outer = jnp.concatenate([pieces[piece * ROWS + row] for row in range(8)], axis=0)
            inner = decay * outer + jnp.where(low, right, left)
            for_left = jnp.where(low, inner, outer)
            for_right = jnp.where(low, outer, inner)
            mine, others = order(first, for_left, for_right)
            keep[piece] = mine
            send[piece] = others
            total[piece : piece + 1, :] = pieces[piece * ROWS + 8]


def final_kernel(
    core, query, key, value, grad, residue, rate, near, back, own, other, mixed, grad_query, grad_key, grad_value, work
):
    length = query.shape[1]
    repeat = query.shape[2] // (2 * LANES)
    first = core[0] == 0
    low = bottom()
    for half in range(2):
        decay, forward, backward = [], [], []
        for n in range(MODES):
            piece = half * MODES + n
            weight = spread(residue[n : n + 1, lanes_of(half)])
            decay.append(spread(jnp.exp(-rate[n : n + 1, lanes_of(half)])))
            one, two = order(first, own[piece], other[piece])
            forward.append(weight * jnp.where(low, swap_halves(two), one))
            backward.append(weight * jnp.where(low, two, swap_halves(one)))

        def step(i, carry, decay=decay, half=half, source=near):
            carry = [decay[n] * carry[n] for n in range(MODES)]
            rows = pl.ds(pl.multiple_of(i * 8, 8), 8)
            work[rows, :] = source[half, rows, :] + tree(carry)
            return tuple(carry)

        lax.fori_loop(0, length, step, tuple(forward), unroll=2)
        for seq in range(2):
            for rep in range(repeat):
                cut = pl.ds(rep * 2 * LANES + half * LANES, LANES)
                z = work[pl.ds(seq * repeat + rep, length, stride=8), :]
                mixed[seq, :, cut] = (query[seq, :, cut].astype(F32) * z).astype(jnp.bfloat16)
                grad_query[seq, :, cut] = (grad[seq, :, cut].astype(F32) * z).astype(jnp.bfloat16)

        def step_back(i, carry, decay=decay, half=half):
            return step(length - 1 - i, carry, decay, half, back)

        lax.fori_loop(0, length, step_back, tuple(backward), unroll=2)
        for seq in range(2):
            for rep in range(repeat):
                cut = pl.ds(rep * 2 * LANES + half * LANES, LANES)
                du = work[pl.ds(seq * repeat + rep, length, stride=8), :]
                grad_key[seq, :, cut] = (du * value[seq, :, cut].astype(F32)).astype(jnp.bfloat16)
                grad_value[seq, :, cut] = (du * key[seq, :, cut].astype(F32)).astype(jnp.bfloat16)


VMEM = pl.BlockSpec(memory_space=pltpu.VMEM)
SMEM = pl.BlockSpec(memory_space=pltpu.SMEM)


def struct(*shape, dtype=F32):
    return jax.ShapeDtypeStruct(shape, dtype)


def local(query, key, value, grad_out, residue, rate):
    seq_count, block, channels = query.shape
    pieces = 2 * MODES
    core_id = lax.axis_index("core")
    core = core_id.astype(jnp.int32).reshape(1)
    tile = struct(pieces, 8, LANES)
    rows = struct(pieces * ROWS, 1, LANES)
    works = struct(2, block * 8, LANES)
    near, back, keep, send, within = pl.pallas_call(
        local_kernel,
        name="local",
        out_shape=(works, works, tile, tile, struct(pieces, LANES)),
        in_specs=[SMEM] + [VMEM] * 6,
        out_specs=(VMEM,) * 5,
        scratch_shapes=[pltpu.VMEM((block * 8, LANES), F32)] * 2,
    )(core, query, key, value, grad_out, residue, rate)
    exchange = [(0, 1), (1, 0)]
    other = lax.ppermute(send, "core", exchange)
    joined = pl.pallas_call(
        functools.partial(pair_kernel, block=block),
        name="pair",
        out_shape=rows,
        in_specs=[SMEM] + [VMEM] * 4,
        out_specs=VMEM,
    )(core, keep, other, within, rate)
    gathered = lax.all_to_all(joined, ("xh", "z"), 0, 0, tiled=True)
    pace = lax.dynamic_slice(
        rate, (lax.axis_index("z"), lax.axis_index("xh") * LANES), (1, LANES)
    )
    scanned = pl.pallas_call(
        functools.partial(scan_kernel, block=2 * block),
        name="scan",
        out_shape=rows,
        in_specs=[VMEM] * 2,
        out_specs=VMEM,
    )(gathered, pace)
    returned = lax.all_to_all(scanned, ("xh", "z"), 0, 0, tiled=True)
    state, state_send, total = pl.pallas_call(
        functools.partial(split_kernel, block=block),
        name="split",
        out_shape=(tile, tile, struct(pieces, LANES)),
        in_specs=[SMEM] + [VMEM] * 4,
        out_specs=(VMEM,) * 3,
    )(core, returned, keep, other, rate)
    state_other = lax.ppermute(state_send, "core", exchange)
    group = lax.axis_size("core") * lax.axis_size("tensor")
    copies = jnp.broadcast_to(total[None], (group,) + total.shape)
    totals = lax.all_to_all(copies, ("core", "tensor"), 0, 0, tiled=True)
    summed = jnp.sum(totals, axis=0)
    summed = jnp.concatenate([summed[:MODES], summed[MODES:]], axis=1)
    length = block * lax.axis_size(("xh", "z", "core"))
    grad_residue = summed / float(seq_count * length)
    whole = struct(*query.shape, dtype=jnp.bfloat16)
    mixed, grad_query, grad_key, grad_value = pl.pallas_call(
        final_kernel,
        name="final",
        out_shape=(whole,) * 4,
        in_specs=[SMEM] + [VMEM] * 10,
        out_specs=(VMEM,) * 4,
        scratch_shapes=[pltpu.VMEM((block * 8, LANES), F32)],
    )(core, query, key, value, grad_out, residue, rate, near, back, state, state_other)
    return (mixed, grad_query, grad_key, grad_value, grad_residue)


def solution(mesh):
    shape = (2, 16, 2, mesh.shape["tensor"])
    split = Mesh(mesh.devices.reshape(shape), ("xh", "z", "core", "tensor"))
    spec = P(None, ("xh", "z", "core"), "tensor")
    specs = (spec, spec, spec, spec)
    return jax.shard_map(
        local, mesh=split, in_specs=specs + (P(), P()), out_specs=specs + (P(),), check_vma=False
    )
```

```python
import functools

import jax
import jax.numpy as jnp
from jax import lax
from jax.experimental import pallas as pl
from jax.experimental.pallas import tpu as pltpu
from jax.sharding import Mesh, PartitionSpec as P

F32 = jnp.float32
LANES = 128
MODES = 16
ROWS = 9


def spread(row):
    return jnp.broadcast_to(row, (8, LANES))


def bottom():
    return lax.broadcasted_iota(jnp.int32, (8, LANES), 0) >= 4


def swap_halves(tile):
    return pltpu.roll(tile, 4, 0)


def lanes_of(half):
    return pl.ds(half * LANES, LANES)


def columns(half, rep):
    return pl.ds(rep * 2 * LANES + half * LANES, LANES)


def slab_copy(source, target, sems, which, half, rep):
    cut = columns(half, rep)
    return pltpu.make_async_copy(source.at[:, :, cut], target.at[:, :, cut], sems.at[which, half, rep])


def fetch(pairs, sems, half, repeat, wait):
    for rep in range(repeat):
        for which, (source, target) in enumerate(pairs):
            copy = slab_copy(source, target, sems, which, half, rep)
            copy.wait() if wait else copy.start()


def products_of(half, first, second, work, repeat):
    length = first.shape[1]
    for seq in range(2):
        for rep in range(repeat):
            cut = columns(half, rep)
            rows = pl.ds(seq * repeat + rep, length, stride=8)
            work[half, rows, :] = first[seq, :, cut].astype(F32) * second[seq, :, cut].astype(F32)


def sums_kernel(
    core,
    query_in,
    key_in,
    value_in,
    grad_in,
    rate,
    keep,
    send,
    within,
    query,
    key,
    value,
    grad,
    work_u,
    work_g,
    sems,
):
    length = query.shape[1]
    repeat = query.shape[2] // (2 * LANES)
    first = core[0] == 0
    pairs = ((key_in, key), (value_in, value), (grad_in, grad), (query_in, query))
    for half in range(2):
        fetch(pairs, sems, half, repeat, False)
    for half in range(2):
        fetch(pairs, sems, half, repeat, True)
        products_of(half, key, value, work_u, repeat)
        products_of(half, grad, query, work_g, repeat)
        for group in range(0, MODES, 8):
            decay = [spread(jnp.exp(-rate[n : n + 1, lanes_of(half)])) for n in range(group, group + 8)]

            def step(i, carry, decay=decay, half=half):
                ups, downs, sums = (list(c) for c in carry)
                ahead = pl.ds(pl.multiple_of(i * 8, 8), 8)
                behind = pl.ds(pl.multiple_of((length - 1 - i) * 8, 8), 8)
                u, g, gr = work_u[half, ahead, :], work_g[half, ahead, :], work_g[half, behind, :]
                for m in range(8):
                    ups[m] = decay[m] * ups[m] + u
                    downs[m] = decay[m] * downs[m] + gr
                    sums[m] = sums[m] + g * ups[m]
                return tuple(ups), tuple(downs), tuple(sums)

            zero = tuple(jnp.zeros((8, LANES), F32) for _ in range(8))
            ups, downs, sums = lax.fori_loop(0, length, step, (zero, zero, zero), unroll=4)
            low = bottom()
            for m in range(8):
                top_half = jnp.where(low, swap_halves(downs[m]), ups[m])
                end_half = jnp.where(low, downs[m], swap_halves(ups[m]))
                piece = half * MODES + group + m
                keep[piece] = jnp.where(first, top_half, end_half)
                send[piece] = jnp.where(first, end_half, top_half)
                within[piece : piece + 1, :] = jnp.sum(sums[m], axis=0, keepdims=True)


def near_kernel(
    query_in, key_in, value_in, grad_in, residue, rate, near, back, query, key, value, grad, work_u, work_g, sems
):
    length = query.shape[1]
    repeat = query.shape[2] // (2 * LANES)
    pairs = ((key_in, key), (value_in, value), (grad_in, grad), (query_in, query))
    for half in range(2):
        fetch(pairs, sems, half, repeat, False)
    for half in range(2):
        fetch(pairs, sems, half, repeat, True)
        products_of(half, key, value, work_u, repeat)
        products_of(half, grad, query, work_g, repeat)
        for group in range(0, MODES, 8):
            modes = range(group, group + 8)
            decay = [spread(jnp.exp(-rate[n : n + 1, lanes_of(half)])) for n in modes]
            weight = [spread(residue[n : n + 1, lanes_of(half)]) for n in modes]

            def step(i, carry, decay=decay, weight=weight, group=group, half=half):
                ups, downs = (list(c) for c in carry)
                ahead = pl.ds(pl.multiple_of(i * 8, 8), 8)
                behind = pl.ds(pl.multiple_of((length - 1 - i) * 8, 8), 8)
                u, g = work_u[half, ahead, :], work_g[half, behind, :]
                for m in range(8):
                    ups[m] = decay[m] * ups[m] + u
                    downs[m] = decay[m] * downs[m] + g
                z = tree([weight[m] * ups[m] for m in range(8)])
                dz = tree([weight[m] * downs[m] for m in range(8)])
                if group:
                    z, dz = z + near[half, ahead, :], dz + back[half, behind, :]
                near[half, ahead, :] = z
                back[half, behind, :] = dz
                return tuple(ups), tuple(downs)

            zero = tuple(jnp.zeros((8, LANES), F32) for _ in range(8))
            lax.fori_loop(0, length, step, (zero, zero), unroll=2)


def tree(parts):
    while len(parts) > 1:
        parts = [parts[i] + parts[i + 1] for i in range(0, len(parts), 2)]
    return parts[0]


def order(first, own, other):
    return jnp.where(first, own, other), jnp.where(first, other, own)


def pair_kernel(core, own, other, within, rate, out, *, block):
    first = core[0] == 0
    low = bottom()
    for half in range(2):
        for n in range(MODES):
            piece = half * MODES + n
            pace = rate[n : n + 1, lanes_of(half)]
            decay = spread(jnp.exp(-pace * float(block)))
            left, right = order(first, own[piece], other[piece])
            joined = jnp.where(low, left + decay * right, decay * left + right)
            cross = jnp.where(low, 0.0, left * swap_halves(right))
            total = jnp.exp(-pace) * jnp.sum(cross, axis=0, keepdims=True)
            for row in range(8):
                out[piece * ROWS + row] = joined[row : row + 1, :]
            out[piece * ROWS + 8] = within[piece : piece + 1, :] + total


def scan_kernel(pieces, pace, out, *, block):
    count = pieces.shape[0] // ROWS
    decay = jnp.exp(-pace[...] * float(block))
    decay4 = jnp.broadcast_to(decay, (4, LANES))

    def load(index, base):
        return jnp.concatenate([pieces[index * ROWS + base + j] for j in range(4)], axis=0)

    ahead = jnp.zeros((4, LANES), F32)
    cross = jnp.zeros((4, LANES), F32)
    local = jnp.zeros((1, LANES), F32)
    for index in range(count):
        for j in range(4):
            out[index * ROWS + j] = ahead[j : j + 1, :]
        cross = cross + ahead * load(index, 4)
        local = local + pieces[index * ROWS + 8]
        ahead = decay4 * ahead + load(index, 0)
    behind = jnp.zeros((4, LANES), F32)
    for index in reversed(range(count)):
        for j in range(4):
            out[index * ROWS + 4 + j] = behind[j : j + 1, :]
        behind = decay4 * behind + load(index, 4)
    total = local + jnp.exp(-pace[...]) * jnp.sum(cross, axis=0, keepdims=True)
    for index in range(count):
        out[index * ROWS + 8] = total


def split_kernel(core, pieces, own, other, rate, keep, send, total, *, block):
    first = core[0] == 0
    low = bottom()
    for half in range(2):
        for n in range(MODES):
            piece = half * MODES + n
            pace = rate[n : n + 1, lanes_of(half)]
            decay = spread(jnp.exp(-pace * float(block)))
            left, right = order(first, own[piece], other[piece])
            outer = jnp.concatenate([pieces[piece * ROWS + row] for row in range(8)], axis=0)
            inner = decay * outer + jnp.where(low, right, left)
            for_left = jnp.where(low, inner, outer)
            for_right = jnp.where(low, outer, inner)
            mine, others = order(first, for_left, for_right)
            keep[piece] = mine
            send[piece] = others
            row = pieces[piece * ROWS + 8]
            for copy in range(total.shape[0]):
                total[copy, piece : piece + 1, :] = row


def final_kernel(
    core,
    query_in,
    key_in,
    value_in,
    grad_in,
    residue,
    rate,
    near,
    back,
    own,
    other,
    mixed_out,
    grad_query_out,
    grad_key_out,
    grad_value_out,
    work,
    query,
    key,
    value,
    grad,
    mixed,
    grad_query,
    grad_key,
    grad_value,
    in_sems,
    sems,
):
    length = query.shape[1]
    repeat = query.shape[2] // (2 * LANES)
    first = core[0] == 0
    low = bottom()
    outs = ((mixed, mixed_out), (grad_query, grad_query_out), (grad_key, grad_key_out), (grad_value, grad_value_out))

    pairs = ((query_in, query), (grad_in, grad), (value_in, value), (key_in, key))
    for half in range(2):
        fetch(pairs, in_sems, half, repeat, False)

    def products(half, source_a, source_b, base):
        target_a, target_b = outs[base][0], outs[base + 1][0]
        for rep in range(repeat):
            cut = columns(half, rep)
            for seq in range(2):
                shared = work[pl.ds(seq * repeat + rep, length, stride=8), :]
                target_a[seq, :, cut] = (source_a[seq, :, cut].astype(F32) * shared).astype(jnp.bfloat16)
                target_b[seq, :, cut] = (source_b[seq, :, cut].astype(F32) * shared).astype(jnp.bfloat16)
            for which in (base, base + 1):
                slab_copy(*outs[which], sems, which, half, rep).start()

    for half in range(2):
        decay, forward, backward = [], [], []
        for n in range(MODES):
            piece = half * MODES + n
            weight = spread(residue[n : n + 1, lanes_of(half)])
            decay.append(spread(jnp.exp(-rate[n : n + 1, lanes_of(half)])))
            one, two = order(first, own[piece], other[piece])
            forward.append(weight * jnp.where(low, swap_halves(two), one))
            backward.append(weight * jnp.where(low, two, swap_halves(one)))

        def step(i, carry, decay=decay, half=half, source=near):
            carry = [decay[n] * carry[n] for n in range(MODES)]
            rows = pl.ds(pl.multiple_of(i * 8, 8), 8)
            work[rows, :] = source[half, rows, :] + tree(carry)
            return tuple(carry)

        def step_back(i, carry, step=step):
            return step(length - 1 - i, carry, source=back)

        lax.fori_loop(0, length, step, tuple(forward), unroll=2)
        fetch(pairs, in_sems, half, repeat, True)
        products(half, query, grad, 0)
        lax.fori_loop(0, length, step_back, tuple(backward), unroll=2)
        products(half, value, key, 2)
    for which in range(4):
        for half in range(2):
            for rep in range(repeat):
                slab_copy(*outs[which], sems, which, half, rep).wait()


VMEM = pl.BlockSpec(memory_space=pltpu.VMEM)
SMEM = pl.BlockSpec(memory_space=pltpu.SMEM)
HBM = pl.BlockSpec(memory_space=pltpu.HBM)


def room(mebibytes):
    return pltpu.CompilerParams(vmem_limit_bytes=int(mebibytes * 2**20))


def struct(*shape, dtype=F32):
    return jax.ShapeDtypeStruct(shape, dtype)


def local(query, key, value, grad_out, residue, rate):
    seq_count, block, channels = query.shape
    pieces = 2 * MODES
    core_id = lax.axis_index("core")
    core = core_id.astype(jnp.int32).reshape(1)
    tile = struct(pieces, 8, LANES)
    rows = struct(pieces * ROWS, 1, LANES)
    works = struct(2, block * 8, LANES)
    whole = struct(*query.shape, dtype=jnp.bfloat16)
    repeat = channels // (2 * LANES)
    inputs = tuple(pltpu.with_memory_space_constraint(x, pltpu.HBM) for x in (query, key, value, grad_out))
    buffers = [pltpu.VMEM(query.shape, jnp.bfloat16)] * 4
    arrivals = [pltpu.SemaphoreType.DMA((4, 2, repeat))]
    keep, send, within = pl.pallas_call(
        sums_kernel,
        name="sums",
        out_shape=(tile, tile, struct(pieces, LANES)),
        in_specs=[SMEM] + [HBM] * 4 + [VMEM],
        out_specs=(VMEM,) * 3,
        scratch_shapes=buffers + [pltpu.VMEM(works.shape, F32)] * 2 + arrivals,
        compiler_params=room(12),
    )(core, *inputs, rate)
    near, back = pl.pallas_call(
        near_kernel,
        name="near",
        out_shape=(works, works),
        in_specs=[HBM] * 4 + [VMEM] * 2,
        out_specs=(VMEM,) * 2,
        scratch_shapes=buffers + [pltpu.VMEM(works.shape, F32)] * 2 + arrivals,
        compiler_params=room(12),
        cost_estimate=pl.CostEstimate(flops=2**26, transcendentals=0, bytes_accessed=2**22),
    )(*inputs, residue, rate)
    exchange = [(0, 1), (1, 0)]
    other = lax.ppermute(send, "core", exchange)
    joined = pl.pallas_call(
        functools.partial(pair_kernel, block=block),
        name="pair",
        out_shape=rows,
        in_specs=[SMEM] + [VMEM] * 4,
        out_specs=VMEM,
        compiler_params=room(4),
    )(core, keep, other, within, rate)
    gathered = lax.all_to_all(joined, ("xh", "z"), 0, 0, tiled=True)
    gathered, near, back = lax.optimization_barrier((gathered, near, back))
    pace = lax.dynamic_slice(
        rate, (lax.axis_index("z"), lax.axis_index("xh") * LANES), (1, LANES)
    )
    scanned = pl.pallas_call(
        functools.partial(scan_kernel, block=2 * block),
        name="scan",
        out_shape=pltpu.VMEM(rows.shape, F32),
        in_specs=[VMEM] * 2,
        out_specs=VMEM,
        compiler_params=room(4),
    )(gathered, pace)
    returned = lax.all_to_all(scanned, ("xh", "z"), 0, 0, tiled=True)
    group = lax.axis_size("core") * lax.axis_size("tensor")
    state, state_send, total = pl.pallas_call(
        functools.partial(split_kernel, block=block),
        name="split",
        out_shape=(tile, tile, struct(group, pieces, LANES)),
        in_specs=[SMEM] + [VMEM] * 4,
        out_specs=(VMEM,) * 3,
        compiler_params=room(4),
    )(core, returned, keep, other, rate)
    state_other = lax.ppermute(state_send, "core", exchange)
    totals = lax.all_to_all(total, ("core", "tensor"), 0, 0, tiled=True)
    summed = jnp.sum(totals, axis=0)
    summed = jnp.concatenate([summed[:MODES], summed[MODES:]], axis=1)
    length = block * lax.axis_size(("xh", "z", "core"))
    grad_residue = summed / float(seq_count * length)
    mixed, grad_query, grad_key, grad_value = pl.pallas_call(
        final_kernel,
        name="final",
        out_shape=(whole,) * 4,
        in_specs=[SMEM] + [HBM] * 4 + [VMEM] * 6,
        out_specs=(HBM,) * 4,
        scratch_shapes=[pltpu.VMEM((block * 8, LANES), F32)] + buffers * 2 + arrivals * 2,
        compiler_params=room(12),
    )(core, *inputs, residue, rate, near, back, state, state_other)
    return (mixed, grad_query, grad_key, grad_value, grad_residue)


def solution(mesh):
    shape = (2, 16, 2, mesh.shape["tensor"])
    split = Mesh(mesh.devices.reshape(shape), ("xh", "z", "core", "tensor"))
    spec = P(None, ("xh", "z", "core"), "tensor")
    specs = (spec, spec, spec, spec)
    return jax.shard_map(
        local, mesh=split, in_specs=specs + (P(), P()), out_specs=specs + (P(),), check_vma=False
    )
```

```python
import functools

import jax
import jax.numpy as jnp
from jax import lax
from jax.experimental import pallas as pl
from jax.experimental.pallas import tpu as pltpu
from jax.sharding import Mesh, PartitionSpec as P

F32 = jnp.float32
LANES = 128
MODES = 16
ROWS = 9


def spread(row):
    return jnp.broadcast_to(row, (8, LANES))


def bottom():
    return lax.broadcasted_iota(jnp.int32, (8, LANES), 0) >= 4


def swap_halves(tile):
    return pltpu.roll(tile, 4, 0)


def lanes_of(half):
    return pl.ds(half * LANES, LANES)


def columns(half, rep):
    return pl.ds(rep * 2 * LANES + half * LANES, LANES)


def slab_copy(source, target, sems, which, half, rep):
    cut = columns(half, rep)
    return pltpu.make_async_copy(source.at[:, :, cut], target.at[:, :, cut], sems.at[which, half, rep])


def fetch(pairs, sems, half, repeat, wait):
    for rep in range(repeat):
        for which, (source, target) in enumerate(pairs):
            copy = slab_copy(source, target, sems, which, half, rep)
            copy.wait() if wait else copy.start()


def products_of(half, first, second, work, repeat):
    length = first.shape[1]
    for seq in range(2):
        for rep in range(repeat):
            cut = columns(half, rep)
            rows = pl.ds(seq * repeat + rep, length, stride=8)
            work[half, rows, :] = first[seq, :, cut].astype(F32) * second[seq, :, cut].astype(F32)


def sums_kernel(
    core,
    query_in,
    key_in,
    value_in,
    grad_in,
    rate_in,
    work_u,
    work_g,
    keep,
    send,
    within,
    query,
    key,
    value,
    grad,
    rate,
    sems,
    rate_sem,
):
    length = query.shape[1]
    repeat = query.shape[2] // (2 * LANES)
    first = core[0] == 0
    pairs = ((key_in, key), (value_in, value), (grad_in, grad), (query_in, query))
    fetch(pairs, sems, 0, repeat, False)
    rates = pltpu.make_async_copy(rate_in, rate, rate_sem)
    rates.start()
    fetch(pairs, sems, 1, repeat, False)
    for half in range(2):
        if half == 0:
            rates.wait()
        fetch(pairs, sems, half, repeat, True)
        products_of(half, key, value, work_u, repeat)
        products_of(half, grad, query, work_g, repeat)
        for group in range(0, MODES, 8):
            decay = [spread(jnp.exp(-rate[n : n + 1, lanes_of(half)])) for n in range(group, group + 8)]

            def step(i, carry, decay=decay, half=half):
                ups, downs, sums = (list(c) for c in carry)
                ahead = pl.ds(pl.multiple_of(i * 8, 8), 8)
                behind = pl.ds(pl.multiple_of((length - 1 - i) * 8, 8), 8)
                u, g, gr = work_u[half, ahead, :], work_g[half, ahead, :], work_g[half, behind, :]
                for m in range(8):
                    ups[m] = decay[m] * ups[m] + u
                    downs[m] = decay[m] * downs[m] + gr
                    sums[m] = sums[m] + g * ups[m]
                return tuple(ups), tuple(downs), tuple(sums)

            zero = tuple(jnp.zeros((8, LANES), F32) for _ in range(8))
            ups, downs, sums = lax.fori_loop(0, length, step, (zero, zero, zero), unroll=4)
            low = bottom()
            for m in range(8):
                top_half = jnp.where(low, swap_halves(downs[m]), ups[m])
                end_half = jnp.where(low, downs[m], swap_halves(ups[m]))
                piece = 2 * (group + m) + half
                keep[piece] = jnp.where(first, top_half, end_half)
                send[piece] = jnp.where(first, end_half, top_half)
                within[piece : piece + 1, :] = jnp.sum(sums[m], axis=0, keepdims=True)


def near_kernel(work_u, work_g, residue, rate, near, back):
    length = near.shape[1] // 8
    for half in range(2):
        decay = [spread(jnp.exp(-rate[n : n + 1, lanes_of(half)])) for n in range(MODES)]
        weight = [spread(residue[n : n + 1, lanes_of(half)]) for n in range(MODES)]
        for source, target, reverse in ((work_u, near, False), (work_g, back, True)):

            def step(i, states, half=half, source=source, target=target, reverse=reverse, decay=decay, weight=weight):
                index = length - 1 - i if reverse else i
                rows = pl.ds(pl.multiple_of(index * 8, 8), 8)
                value = source[half, rows, :]
                states = tuple(decay[n] * states[n] + value for n in range(MODES))
                target[half, rows, :] = tree([weight[n] * states[n] for n in range(MODES)])
                return states

            lax.fori_loop(0, length, step, tuple(jnp.zeros((8, LANES), F32) for _ in range(MODES)), unroll=2)


def tree(parts):
    while len(parts) > 1:
        parts = [parts[i] + parts[i + 1] for i in range(0, len(parts), 2)]
    return parts[0]


def order(first, own, other):
    return jnp.where(first, own, other), jnp.where(first, other, own)


def pair_kernel(core, own, other, within, rate, out, *, block):
    first = core[0] == 0
    low = bottom()
    for half in range(2):
        for n in range(MODES):
            piece = 2 * n + half
            pace = rate[n : n + 1, lanes_of(half)]
            decay = spread(jnp.exp(-pace * float(block)))
            left, right = order(first, own[piece], other[piece])
            joined = jnp.where(low, left + decay * right, decay * left + right)
            cross = jnp.where(low, 0.0, left * swap_halves(right))
            total = jnp.exp(-pace) * jnp.sum(cross, axis=0, keepdims=True)
            for row in range(8):
                out[piece * ROWS + row] = joined[row : row + 1, :]
            out[piece * ROWS + 8] = within[piece : piece + 1, :] + total


def rows_of(pieces, chip, half, base):
    start = (2 * chip + half) * ROWS + base
    return jnp.concatenate([pieces[start + j] for j in range(4)], axis=0)


def totals_kernel(part, pieces, pace, out, *, block):
    count = pieces.shape[0] // (2 * ROWS)
    early = part[0] == 0
    for half in range(2):
        rates = pace[:, lanes_of(half)]
        decay = jnp.broadcast_to(jnp.exp(-rates * float(block)), (4, LANES))
        ahead, cross, behind = (jnp.zeros((4, LANES), F32) for _ in range(3))
        local = jnp.zeros((1, LANES), F32)
        for chip in range(count):
            cross = cross + ahead * rows_of(pieces, chip, half, 4)
            local = local + pieces[(2 * chip + half) * ROWS + 8]
            ahead = decay * ahead + rows_of(pieces, chip, half, 0)
        for chip in reversed(range(count)):
            behind = decay * behind + rows_of(pieces, chip, half, 4)
        total = local + jnp.exp(-rates) * jnp.sum(cross, axis=0, keepdims=True)
        out[half, 0:4, :] = jnp.where(early, ahead, behind)
        out[half, 4:8, :] = jnp.broadcast_to(total, (4, LANES))


def scan_kernel(part, pieces, pace, own, other, out, *, block):
    count = pieces.shape[0] // (2 * ROWS)
    early = part[0] == 0
    for half in range(2):
        rates = pace[:, lanes_of(half)]
        decay = jnp.broadcast_to(jnp.exp(-rates * float(block)), (4, LANES))
        given = other[half, 0:4, :]
        ahead = jnp.where(early, 0.0, given)
        behind = jnp.where(early, given, 0.0)
        cross = jnp.sum(own[half, 0:4, :] * given, axis=0, keepdims=True)
        total = own[half, 4:5, :] + other[half, 4:5, :] + jnp.exp(-rates) * cross
        for chip in range(count):
            start = (2 * chip + half) * ROWS
            for j in range(4):
                out[start + j] = ahead[j : j + 1, :]
            out[start + 8] = total
            ahead = decay * ahead + rows_of(pieces, chip, half, 0)
        for chip in reversed(range(count)):
            start = (2 * chip + half) * ROWS + 4
            for j in range(4):
                out[start + j] = behind[j : j + 1, :]
            behind = decay * behind + rows_of(pieces, chip, half, 4)


def split_kernel(core, pieces, own, other, rate, keep, send, total, *, block):
    first = core[0] == 0
    low = bottom()
    for half in range(2):
        for n in range(MODES):
            piece = 2 * n + half
            pace = rate[n : n + 1, lanes_of(half)]
            decay = spread(jnp.exp(-pace * float(block)))
            left, right = order(first, own[piece], other[piece])
            outer = jnp.concatenate([pieces[piece * ROWS + row] for row in range(8)], axis=0)
            inner = decay * outer + jnp.where(low, right, left)
            for_left = jnp.where(low, inner, outer)
            for_right = jnp.where(low, outer, inner)
            mine, others = order(first, for_left, for_right)
            keep[piece] = mine
            send[piece] = others
            row = pieces[piece * ROWS + 8]
            for copy in range(total.shape[0]):
                total[copy, half * MODES + n : half * MODES + n + 1, :] = row


def final_kernel(
    core,
    query_in,
    key_in,
    value_in,
    grad_in,
    residue,
    rate,
    near,
    back,
    own,
    other,
    mixed_out,
    grad_query_out,
    grad_key_out,
    grad_value_out,
    work,
    query,
    key,
    value,
    grad,
    mixed,
    grad_query,
    grad_key,
    grad_value,
    in_sems,
    sems,
):
    length = query.shape[1]
    repeat = query.shape[2] // (2 * LANES)
    first = core[0] == 0
    low = bottom()
    outs = ((mixed, mixed_out), (grad_query, grad_query_out), (grad_key, grad_key_out), (grad_value, grad_value_out))

    pairs = ((query_in, query), (grad_in, grad), (value_in, value), (key_in, key))
    for half in range(2):
        fetch(pairs, in_sems, half, repeat, False)

    def products(half, source_a, source_b, base):
        target_a, target_b = outs[base][0], outs[base + 1][0]
        for rep in range(repeat):
            cut = columns(half, rep)
            for seq in range(2):
                shared = work[pl.ds(seq * repeat + rep, length, stride=8), :]
                target_a[seq, :, cut] = (source_a[seq, :, cut].astype(F32) * shared).astype(jnp.bfloat16)
                target_b[seq, :, cut] = (source_b[seq, :, cut].astype(F32) * shared).astype(jnp.bfloat16)
            for which in (base, base + 1):
                slab_copy(*outs[which], sems, which, half, rep).start()

    for half in range(2):
        decay, forward, backward = [], [], []
        for n in range(MODES):
            piece = 2 * n + half
            weight = spread(residue[n : n + 1, lanes_of(half)])
            decay.append(spread(jnp.exp(-rate[n : n + 1, lanes_of(half)])))
            one, two = order(first, own[piece], other[piece])
            forward.append(weight * jnp.where(low, swap_halves(two), one))
            backward.append(weight * jnp.where(low, two, swap_halves(one)))

        def step(i, carry, decay=decay, half=half, source=near):
            carry = [decay[n] * carry[n] for n in range(MODES)]
            rows = pl.ds(pl.multiple_of(i * 8, 8), 8)
            work[rows, :] = source[half, rows, :] + tree(carry)
            return tuple(carry)

        def step_back(i, carry, step=step):
            return step(length - 1 - i, carry, source=back)

        lax.fori_loop(0, length, step, tuple(forward), unroll=2)
        fetch(pairs, in_sems, half, repeat, True)
        products(half, query, grad, 0)
        lax.fori_loop(0, length, step_back, tuple(backward), unroll=2)
        products(half, value, key, 2)
    for which in range(4):
        for half in range(2):
            for rep in range(repeat):
                slab_copy(*outs[which], sems, which, half, rep).wait()


VMEM = pl.BlockSpec(memory_space=pltpu.VMEM)
SMEM = pl.BlockSpec(memory_space=pltpu.SMEM)
HBM = pl.BlockSpec(memory_space=pltpu.HBM)


def room(mebibytes):
    return pltpu.CompilerParams(vmem_limit_bytes=int(mebibytes * 2**20))


def struct(*shape, dtype=F32):
    return jax.ShapeDtypeStruct(shape, dtype)


def staged(query, key, value, grad_out, residue, rate):
    seq_count, block, channels = query.shape
    pieces = 2 * MODES
    core = lax.axis_index("core").astype(jnp.int32).reshape(1)
    part = lax.axis_index("xh").astype(jnp.int32).reshape(1)
    tile = struct(pieces, 8, LANES)
    rows = struct(pieces * ROWS, 1, LANES)
    works = struct(2, block * 8, LANES)
    whole = struct(*query.shape, dtype=jnp.bfloat16)
    repeat = channels // (2 * LANES)
    inputs = tuple(pltpu.with_memory_space_constraint(x, pltpu.HBM) for x in (query, key, value, grad_out))
    buffers = [pltpu.VMEM(query.shape, jnp.bfloat16)] * 4
    arrivals = [pltpu.SemaphoreType.DMA((4, 2, repeat))]
    work_u, work_g, keep, send, within = pl.pallas_call(
        sums_kernel,
        name="sums",
        out_shape=(works, works, tile, tile, struct(pieces, LANES)),
        in_specs=[SMEM] + [HBM] * 5,
        out_specs=(VMEM,) * 5,
        scratch_shapes=buffers + [pltpu.VMEM(rate.shape, F32)] + arrivals + [pltpu.SemaphoreType.DMA],
        compiler_params=room(12),
    )(core, *inputs, pltpu.with_memory_space_constraint(rate, pltpu.HBM))
    near, back = pl.pallas_call(
        near_kernel,
        name="near",
        out_shape=(works, works),
        in_specs=[VMEM] * 4,
        out_specs=(VMEM,) * 2,
        input_output_aliases={0: 0, 1: 1},
        compiler_params=room(12),
        cost_estimate=pl.CostEstimate(flops=2**26, transcendentals=0, bytes_accessed=2**22),
    )(work_u, work_g, residue, rate)
    exchange = [(0, 1), (1, 0)]
    other = lax.ppermute(send, "core", exchange)
    joined = pl.pallas_call(
        functools.partial(pair_kernel, block=block),
        name="pair",
        out_shape=rows,
        in_specs=[SMEM] + [VMEM] * 4,
        out_specs=VMEM,
        compiler_params=room(4),
    )(core, keep, other, within, rate)
    gathered = lax.all_to_all(joined, "z", 0, 0, tiled=True)
    gathered, near, back = lax.optimization_barrier((gathered, near, back))
    pace = lax.dynamic_slice(rate, (lax.axis_index("z"), 0), (1, rate.shape[1]))
    totals = pl.pallas_call(
        functools.partial(totals_kernel, block=2 * block),
        name="totals",
        out_shape=struct(2, 8, LANES),
        in_specs=[SMEM] + [VMEM] * 2,
        out_specs=VMEM,
        compiler_params=room(4),
    )(part, gathered, pace)
    totals_other = lax.ppermute(totals, "xh", exchange)
    scanned = pl.pallas_call(
        functools.partial(scan_kernel, block=2 * block),
        name="scan",
        out_shape=pltpu.VMEM(rows.shape, F32),
        in_specs=[SMEM] + [VMEM] * 4,
        out_specs=VMEM,
        compiler_params=room(4),
    )(part, gathered, pace, totals, totals_other)
    returned = lax.all_to_all(scanned, "z", 0, 0, tiled=True)
    group = lax.axis_size("core") * lax.axis_size("tensor")
    state, state_send, total = pl.pallas_call(
        functools.partial(split_kernel, block=block),
        name="split",
        out_shape=(tile, tile, struct(group, pieces, LANES)),
        in_specs=[SMEM] + [VMEM] * 4,
        out_specs=(VMEM,) * 3,
        compiler_params=room(4),
    )(core, returned, keep, other, rate)
    state_other = lax.ppermute(state_send, "core", exchange)
    shares = lax.all_to_all(total, ("core", "tensor"), 0, 0, tiled=True)
    summed = jnp.sum(shares, axis=0)
    length = block * lax.axis_size(("xh", "z", "core"))
    summed = jnp.concatenate([summed[:MODES], summed[MODES:]], axis=1)
    grad_residue = summed / float(seq_count * length)
    mixed, grad_query, grad_key, grad_value = pl.pallas_call(
        final_kernel,
        name="final",
        out_shape=(whole,) * 4,
        in_specs=[SMEM] + [HBM] * 4 + [VMEM] * 6,
        out_specs=(HBM,) * 4,
        scratch_shapes=[pltpu.VMEM((block * 8, LANES), F32)] + buffers * 2 + arrivals * 2,
        compiler_params=room(12),
    )(core, *inputs, residue, rate, near, back, state, state_other)
    return (mixed, grad_query, grad_key, grad_value, grad_residue)


def solution(mesh):
    shape = (2, 16, 2, mesh.shape["tensor"])
    split = Mesh(mesh.devices.reshape(shape), ("xh", "z", "core", "tensor"))
    spec = P(None, ("xh", "z", "core"), "tensor")
    specs = (spec, spec, spec, spec)
    return jax.shard_map(staged, mesh=split, in_specs=specs + (P(), P()), out_specs=specs + (P(),), check_vma=False)
```

```python
import functools

import jax
import jax.numpy as jnp
from jax import lax
from jax.experimental import pallas as pl
from jax.experimental.pallas import tpu as pltpu
from jax.sharding import Mesh, PartitionSpec as P

F32 = jnp.float32
LANES = 128
MODES = 16
STEP = 4
WAVE = 4
SHARE = 10
ROWS = 9


def spread(row):
    return jnp.broadcast_to(row, (8, LANES))


def first_core(seat, members):
    return lax.rem(seat[0], members // 2) < members // 4


def bottom():
    return lax.broadcasted_iota(jnp.int32, (8, LANES), 0) >= 4


def swap_halves(tile):
    return pltpu.roll(tile, 4, 0)


def lanes_of(half):
    return pl.ds(half * LANES, LANES)


def columns(half, rep):
    return pl.ds(rep * 2 * LANES + half * LANES, LANES)


def slab_copy(source, target, sems, which, half, rep):
    cut = columns(half, rep)
    return pltpu.make_async_copy(source.at[:, :, cut], target.at[:, :, cut], sems.at[which, half, rep])


def fetch(pairs, sems, half, repeat, wait):
    for rep in range(repeat):
        for which, (source, target) in enumerate(pairs):
            copy = slab_copy(source, target, sems, which, half, rep)
            copy.wait() if wait else copy.start()


def products_of(half, first, second, work, repeat):
    length = first.shape[1]
    for seq in range(2):
        for rep in range(repeat):
            cut = columns(half, rep)
            rows = pl.ds(seq * repeat + rep, length, stride=8)
            work[half, rows, :] = first[seq, :, cut].astype(F32) * second[seq, :, cut].astype(F32)


def sums_kernel(
    seat,
    query_in,
    key_in,
    value_in,
    grad_in,
    rate_in,
    work_u,
    work_g,
    keep,
    send,
    within,
    query,
    key,
    value,
    grad,
    rate,
    sems,
    rate_sem,
    *,
    members,
):
    length = query.shape[1]
    repeat = query.shape[2] // (2 * LANES)
    first = first_core(seat, members)
    pairs = ((key_in, key), (value_in, value), (grad_in, grad), (query_in, query))
    fetch(pairs, sems, 0, repeat, False)
    rates = pltpu.make_async_copy(rate_in, rate, rate_sem)
    rates.start()
    fetch(pairs, sems, 1, repeat, False)
    for half in range(2):
        if half == 0:
            rates.wait()
        fetch(pairs, sems, half, repeat, True)
        products_of(half, key, value, work_u, repeat)
        products_of(half, grad, query, work_g, repeat)
        lags = None
        for group in range(0, MODES, WAVE):
            modes = range(group, group + WAVE)
            decay = [spread(jnp.exp(-rate[n : n + 1, lanes_of(half)])) for n in modes]
            jump = [spread(jnp.exp(-rate[n : n + 1, lanes_of(half)] * float(STEP))) for n in modes]

            def step(i, carry, decay=decay, jump=jump, half=half):
                ups, downs, powers, sums, pairs = (list(c) for c in carry)
                base = i * (8 * STEP)
                rows = [pl.ds(pl.multiple_of(base + 8 * j, 8), 8) for j in range(STEP)]
                us = [work_u[half, row, :] for row in rows]
                gs = [work_g[half, row, :] for row in rows]
                for lag in range(len(pairs)):
                    for j in range(lag, STEP):
                        pairs[lag] = pairs[lag] + gs[j] * us[j - lag]
                for m in range(WAVE):
                    risen, fallen = us[0], gs[-1]
                    for j in range(1, STEP):
                        risen = decay[m] * risen + us[j]
                        fallen = decay[m] * fallen + gs[STEP - 1 - j]
                    sums[m] = sums[m] + fallen * ups[m]
                    ups[m] = jump[m] * ups[m] + risen
                    downs[m] = downs[m] + powers[m] * fallen
                    powers[m] = powers[m] * jump[m]
                return tuple(ups), tuple(downs), tuple(powers), tuple(sums), tuple(pairs)

            zero = tuple(jnp.zeros((8, LANES), F32) for _ in range(WAVE))
            ones = tuple(jnp.ones((8, LANES), F32) for _ in range(WAVE))
            none = () if lags else tuple(jnp.zeros((8, LANES), F32) for _ in range(STEP))
            ups, downs, _, sums, pairs_of = lax.fori_loop(
                0, length // STEP, step, (zero, zero, ones, zero, none), unroll=2
            )
            lags = lags or pairs_of
            low = bottom()
            for m in range(WAVE):
                top_half = jnp.where(low, swap_halves(downs[m]), ups[m])
                end_half = jnp.where(low, downs[m], swap_halves(ups[m]))
                piece = 2 * (group + m) + half
                keep[piece] = jnp.where(first, top_half, end_half)
                send[piece] = jnp.where(first, end_half, top_half)
                inner = lags[-1]
                for lag in reversed(range(STEP - 1)):
                    inner = decay[m] * inner + lags[lag]
                inner = inner + decay[m] * sums[m]
                within[piece : piece + 1, :] = jnp.sum(inner, axis=0, keepdims=True)


def near_kernel(work_u, work_g, residue, rate, near, back):
    length = near.shape[1] // 8
    for half in range(2):
        decay = [spread(jnp.exp(-rate[n : n + 1, lanes_of(half)])) for n in range(MODES)]
        weight = [spread(residue[n : n + 1, lanes_of(half)]) for n in range(MODES)]
        for source, target, reverse in ((work_u, near, False), (work_g, back, True)):

            def step(i, states, half=half, source=source, target=target, reverse=reverse, decay=decay, weight=weight):
                index = length - 1 - i if reverse else i
                rows = pl.ds(pl.multiple_of(index * 8, 8), 8)
                value = source[half, rows, :]
                states = tuple(decay[n] * states[n] + value for n in range(MODES))
                target[half, rows, :] = tree([weight[n] * states[n] for n in range(MODES)])
                return states

            lax.fori_loop(0, length, step, tuple(jnp.zeros((8, LANES), F32) for _ in range(MODES)), unroll=2)


def tree(parts):
    while len(parts) > 1:
        parts = [parts[i] + parts[i + 1] for i in range(0, len(parts), 2)]
    return parts[0]


def order(first, own, other):
    return jnp.where(first, own, other), jnp.where(first, other, own)


def pair_kernel(seat, own, other, within, rate, out, *, block, members):
    first = first_core(seat, members)
    low = bottom()
    for half in range(2):
        for n in range(MODES):
            piece = 2 * n + half
            pace = rate[n : n + 1, lanes_of(half)]
            decay = spread(jnp.exp(-pace * float(block)))
            left, right = order(first, own[piece], other[piece])
            joined = jnp.where(low, left + decay * right, decay * left + right)
            cross = jnp.where(low, 0.0, left * swap_halves(right))
            total = jnp.exp(-pace) * jnp.sum(cross, axis=0, keepdims=True)
            for row in range(8):
                out[piece * ROWS + row] = joined[row : row + 1, :]
            out[piece * ROWS + 8] = within[piece : piece + 1, :] + total


def rows_of(pieces, chip, half, base):
    start = (2 * chip + half) * ROWS + base
    return jnp.concatenate([pieces[start + j] for j in range(4)], axis=0)


def totals_kernel(seat, pieces, pace, out, *, block, members):
    count = pieces.shape[0] // (2 * ROWS)
    early = seat[0] < members // 2
    for half in range(2):
        rates = pace[:, lanes_of(half)]
        decay = jnp.broadcast_to(jnp.exp(-rates * float(block)), (4, LANES))
        ahead, cross, behind = (jnp.zeros((4, LANES), F32) for _ in range(3))
        local = jnp.zeros((1, LANES), F32)
        for chip in range(count):
            cross = cross + ahead * rows_of(pieces, chip, half, 4)
            local = local + pieces[(2 * chip + half) * ROWS + 8]
            ahead = decay * ahead + rows_of(pieces, chip, half, 0)
        for chip in reversed(range(count)):
            behind = decay * behind + rows_of(pieces, chip, half, 4)
        total = local + jnp.exp(-rates) * jnp.sum(cross, axis=0, keepdims=True)
        shown = jnp.where(early, ahead, behind)
        for copy in range(out.shape[0] // SHARE):
            for j in range(4):
                out[copy * SHARE + 4 * half + j] = shown[j : j + 1, :]
            out[copy * SHARE + 8 + half] = total


def scan_kernel(seat, pieces, pace, shares, out, *, block, members):
    count = pieces.shape[0] // (2 * ROWS)
    pairs = shares.shape[0] // (2 * SHARE)
    early = seat[0] < members // 2
    source = lax.rem(seat[0] + members // 2, members) * SHARE
    for half in range(2):
        rates = pace[:, lanes_of(half)]
        decay = jnp.broadcast_to(jnp.exp(-rates * float(block)), (4, LANES))
        given = jnp.concatenate([shares[source + 4 * half + j] for j in range(4)], axis=0)
        ahead = jnp.where(early, 0.0, given)
        behind = jnp.where(early, given, 0.0)
        cross = jnp.zeros((1, LANES), F32)
        total = jnp.zeros((1, LANES), F32)
        for one in range(pairs):
            two = one + pairs
            total = total + (shares[one * SHARE + 8 + half] + shares[two * SHARE + 8 + half])
            for j in range(4 * half, 4 * half + 4):
                cross = cross + shares[one * SHARE + j] * shares[two * SHARE + j]
        total = total + jnp.exp(-rates) * cross
        for chip in range(count):
            start = (2 * chip + half) * ROWS
            for j in range(4):
                out[start + j] = ahead[j : j + 1, :]
            out[start + 8] = total
            ahead = decay * ahead + rows_of(pieces, chip, half, 0)
        for chip in reversed(range(count)):
            start = (2 * chip + half) * ROWS + 4
            for j in range(4):
                out[start + j] = behind[j : j + 1, :]
            behind = decay * behind + rows_of(pieces, chip, half, 4)


def split_kernel(seat, pieces, own, other, rate, keep, send, *, block, members):
    first = first_core(seat, members)
    low = bottom()
    for half in range(2):
        for n in range(MODES):
            piece = 2 * n + half
            pace = rate[n : n + 1, lanes_of(half)]
            decay = spread(jnp.exp(-pace * float(block)))
            left, right = order(first, own[piece], other[piece])
            outer = jnp.concatenate([pieces[piece * ROWS + row] for row in range(8)], axis=0)
            inner = decay * outer + jnp.where(low, right, left)
            for_left = jnp.where(low, inner, outer)
            for_right = jnp.where(low, outer, inner)
            mine, others = order(first, for_left, for_right)
            keep[piece] = mine
            send[piece] = others


def final_kernel(
    seat,
    query,
    key,
    value,
    grad,
    residue,
    rate,
    near,
    back,
    own,
    other,
    pieces,
    mixed_out,
    grad_query_out,
    grad_key_out,
    grad_value_out,
    grad_residue_out,
    work,
    mixed,
    grad_query,
    grad_key,
    grad_value,
    grad_residue,
    sems,
    residue_sem,
    *,
    scale,
    members,
):
    length = query.shape[1]
    repeat = query.shape[2] // (2 * LANES)
    first = first_core(seat, members)
    low = bottom()
    outs = ((mixed, mixed_out), (grad_query, grad_query_out), (grad_key, grad_key_out), (grad_value, grad_value_out))

    for half in range(2):
        for n in range(MODES):
            grad_residue[n : n + 1, lanes_of(half)] = pieces[(2 * n + half) * ROWS + 8] * scale
    residue_copy = pltpu.make_async_copy(grad_residue, grad_residue_out, residue_sem)
    residue_copy.start()

    def products(half, source_a, source_b, base):
        target_a, target_b = outs[base][0], outs[base + 1][0]
        for rep in range(repeat):
            cut = columns(half, rep)
            for seq in range(2):
                shared = work[pl.ds(seq * repeat + rep, length, stride=8), :]
                target_a[seq, :, cut] = (source_a[seq, :, cut].astype(F32) * shared).astype(jnp.bfloat16)
                target_b[seq, :, cut] = (source_b[seq, :, cut].astype(F32) * shared).astype(jnp.bfloat16)
            for which in (base, base + 1):
                slab_copy(*outs[which], sems, which, half, rep).start()

    for half in range(2):
        decay, forward, backward = [], [], []
        for n in range(MODES):
            piece = 2 * n + half
            weight = spread(residue[n : n + 1, lanes_of(half)])
            decay.append(spread(jnp.exp(-rate[n : n + 1, lanes_of(half)])))
            one, two = order(first, own[piece], other[piece])
            forward.append(weight * jnp.where(low, swap_halves(two), one))
            backward.append(weight * jnp.where(low, two, swap_halves(one)))

        def step(i, carry, decay=decay, half=half, source=near):
            carry = [decay[n] * carry[n] for n in range(MODES)]
            rows = pl.ds(pl.multiple_of(i * 8, 8), 8)
            work[rows, :] = source[half, rows, :] + tree(carry)
            return tuple(carry)

        def step_back(i, carry, step=step):
            return step(length - 1 - i, carry, source=back)

        lax.fori_loop(0, length, step, tuple(forward), unroll=2)
        products(half, query, grad, 0)
        lax.fori_loop(0, length, step_back, tuple(backward), unroll=2)
        products(half, value, key, 2)
    for which in range(4):
        for half in range(2):
            for rep in range(repeat):
                slab_copy(*outs[which], sems, which, half, rep).wait()
    residue_copy.wait()


VMEM = pl.BlockSpec(memory_space=pltpu.VMEM)
SMEM = pl.BlockSpec(memory_space=pltpu.SMEM)
HBM = pl.BlockSpec(memory_space=pltpu.HBM)


def room(mebibytes):
    return pltpu.CompilerParams(vmem_limit_bytes=int(mebibytes * 2**20))


def struct(*shape, dtype=F32):
    return jax.ShapeDtypeStruct(shape, dtype)


def local(query, key, value, grad_out, residue, rate):
    seq_count, block, channels = query.shape
    pieces = 2 * MODES
    owners = ("xh", "core", "tensor")
    members = lax.axis_size(owners)
    seat = lax.axis_index(owners).astype(jnp.int32).reshape(1)
    tile = struct(pieces, 8, LANES)
    rows = struct(pieces * ROWS, 1, LANES)
    works = struct(2, block * 8, LANES)
    whole = struct(*query.shape, dtype=jnp.bfloat16)
    repeat = channels // (2 * LANES)
    inputs = tuple(pltpu.with_memory_space_constraint(x, pltpu.HBM) for x in (query, key, value, grad_out))
    buffers = [pltpu.VMEM(query.shape, jnp.bfloat16)] * 4
    arrivals = [pltpu.SemaphoreType.DMA((4, 2, repeat))]
    work_u, work_g, keep, send, within = pl.pallas_call(
        functools.partial(sums_kernel, members=members),
        name="sums",
        out_shape=(works, works, tile, tile, struct(pieces, LANES)),
        in_specs=[SMEM] + [HBM] * 5,
        out_specs=(VMEM,) * 5,
        scratch_shapes=buffers + [pltpu.VMEM(rate.shape, F32)] + arrivals + [pltpu.SemaphoreType.DMA],
        compiler_params=room(12),
    )(seat, *inputs, pltpu.with_memory_space_constraint(rate, pltpu.HBM))
    near, back = pl.pallas_call(
        near_kernel,
        name="near",
        out_shape=(works, works),
        in_specs=[VMEM] * 4,
        out_specs=(VMEM,) * 2,
        input_output_aliases={0: 0, 1: 1},
        compiler_params=room(12),
        cost_estimate=pl.CostEstimate(flops=2**26, transcendentals=0, bytes_accessed=2**22),
    )(work_u, work_g, residue, rate)
    exchange = [(0, 1), (1, 0)]
    other = lax.ppermute(send, "core", exchange)
    joined = pl.pallas_call(
        functools.partial(pair_kernel, block=block, members=members),
        name="pair",
        out_shape=rows,
        in_specs=[SMEM] + [VMEM] * 4,
        out_specs=VMEM,
        compiler_params=room(4),
    )(seat, keep, other, within, rate)
    gathered = lax.all_to_all(joined, "z", 0, 0, tiled=True)
    gathered, near, back = lax.optimization_barrier((gathered, near, back))
    pace = lax.dynamic_slice(rate, (lax.axis_index("z"), 0), (1, rate.shape[1]))
    shown = pl.pallas_call(
        functools.partial(totals_kernel, block=2 * block, members=members),
        name="totals",
        out_shape=pltpu.VMEM((members * SHARE, 1, LANES), F32),
        in_specs=[SMEM] + [VMEM] * 2,
        out_specs=VMEM,
        compiler_params=room(4),
    )(seat, gathered, pace)
    shares = lax.all_to_all(shown, owners, 0, 0, tiled=True)
    scanned = pl.pallas_call(
        functools.partial(scan_kernel, block=2 * block, members=members),
        name="scan",
        out_shape=pltpu.VMEM(rows.shape, F32),
        in_specs=[SMEM] + [VMEM] * 3,
        out_specs=VMEM,
        compiler_params=room(4),
    )(seat, gathered, pace, shares)
    returned = lax.all_to_all(scanned, "z", 0, 0, tiled=True)
    state, state_send = pl.pallas_call(
        functools.partial(split_kernel, block=block, members=members),
        name="split",
        out_shape=(tile, tile),
        in_specs=[SMEM] + [VMEM] * 4,
        out_specs=(VMEM,) * 2,
        compiler_params=room(4),
    )(seat, returned, keep, other, rate)
    state_other = lax.ppermute(state_send, "core", exchange)
    length = block * lax.axis_size(("xh", "z", "core"))
    return pl.pallas_call(
        functools.partial(final_kernel, scale=1.0 / float(seq_count * length), members=members),
        name="final",
        out_shape=(whole,) * 4 + (struct(*residue.shape),),
        in_specs=[SMEM] + [VMEM] * 11,
        out_specs=(HBM,) * 5,
        scratch_shapes=[pltpu.VMEM((block * 8, LANES), F32)]
        + buffers
        + [pltpu.VMEM(residue.shape, F32)]
        + arrivals
        + [pltpu.SemaphoreType.DMA],
        compiler_params=room(12),
    )(seat, query, key, value, grad_out, residue, rate, near, back, state, state_other, returned)


def solution(mesh):
    shape = (2, 16, 2, mesh.shape["tensor"])
    split = Mesh(mesh.devices.reshape(shape), ("xh", "z", "core", "tensor"))
    spec = P(None, ("xh", "z", "core"), "tensor")
    specs = (spec, spec, spec, spec)
    return jax.shard_map(
        local, mesh=split, in_specs=specs + (P(), P()), out_specs=specs + (P(),), check_vma=False
    )
```

```python
import functools

import jax
import jax.numpy as jnp
from jax import lax
from jax.experimental import pallas as pl
from jax.experimental.pallas import tpu as pltpu
from jax.sharding import Mesh, PartitionSpec as P

F32 = jnp.float32
LANES = 128
MODES = 16
STEP = 4
WAVE = 4
ROWS = 9


def spread(row):
    return jnp.broadcast_to(row, (8, LANES))


def bottom():
    return lax.broadcasted_iota(jnp.int32, (8, LANES), 0) >= 4


def swap_halves(tile):
    return pltpu.roll(tile, 4, 0)


def lanes_of(half):
    return pl.ds(half * LANES, LANES)


def columns(half, rep):
    return pl.ds(rep * 2 * LANES + half * LANES, LANES)


def slab_copy(source, target, sems, which, half, rep):
    cut = columns(half, rep)
    return pltpu.make_async_copy(source.at[:, :, cut], target.at[:, :, cut], sems.at[which, half, rep])


def fetch(pairs, sems, half, repeat, wait, base=0):
    for rep in range(repeat):
        for which, (source, target) in enumerate(pairs):
            copy = slab_copy(source, target, sems, base + which, half, rep)
            copy.wait() if wait else copy.start()


def products_of(half, first, second, work, repeat):
    length = first.shape[1]
    for seq in range(2):
        for rep in range(repeat):
            cut = columns(half, rep)
            rows = pl.ds(seq * repeat + rep, length, stride=8)
            work[half, rows, :] = first[seq, :, cut].astype(F32) * second[seq, :, cut].astype(F32)


def sums_kernel(
    core,
    query_in,
    key_in,
    value_in,
    grad_in,
    rate_in,
    work_u,
    work_g,
    keep,
    send,
    within,
    query,
    key,
    value,
    grad,
    rate,
    sems,
    rate_sem,
):
    length = query.shape[1]
    repeat = query.shape[2] // (2 * LANES)
    first = core[0] == 0
    pairs = ((key_in, key), (value_in, value), (grad_in, grad), (query_in, query))
    fetch(pairs, sems, 0, repeat, False)
    rates = pltpu.make_async_copy(rate_in, rate, rate_sem)
    rates.start()
    fetch(pairs, sems, 1, repeat, False)
    for half in range(2):
        if half == 0:
            rates.wait()
        fetch(pairs, sems, half, repeat, True)
        products_of(half, key, value, work_u, repeat)
        products_of(half, grad, query, work_g, repeat)
        lags = None
        for group in range(0, MODES, WAVE):
            modes = range(group, group + WAVE)
            decay = [spread(jnp.exp(-rate[n : n + 1, lanes_of(half)])) for n in modes]
            jump = [spread(jnp.exp(-rate[n : n + 1, lanes_of(half)] * float(STEP))) for n in modes]

            def step(i, carry, decay=decay, jump=jump, half=half):
                ups, downs, powers, sums, pairs = (list(c) for c in carry)
                base = i * (8 * STEP)
                rows = [pl.ds(pl.multiple_of(base + 8 * j, 8), 8) for j in range(STEP)]
                us = [work_u[half, row, :] for row in rows]
                gs = [work_g[half, row, :] for row in rows]
                for lag in range(len(pairs)):
                    for j in range(lag, STEP):
                        pairs[lag] = pairs[lag] + gs[j] * us[j - lag]
                for m in range(WAVE):
                    risen, fallen = us[0], gs[-1]
                    for j in range(1, STEP):
                        risen = decay[m] * risen + us[j]
                        fallen = decay[m] * fallen + gs[STEP - 1 - j]
                    sums[m] = sums[m] + fallen * ups[m]
                    ups[m] = jump[m] * ups[m] + risen
                    downs[m] = downs[m] + powers[m] * fallen
                    powers[m] = powers[m] * jump[m]
                return tuple(ups), tuple(downs), tuple(powers), tuple(sums), tuple(pairs)

            zero = tuple(jnp.zeros((8, LANES), F32) for _ in range(WAVE))
            ones = tuple(jnp.ones((8, LANES), F32) for _ in range(WAVE))
            none = () if lags else tuple(jnp.zeros((8, LANES), F32) for _ in range(STEP))
            ups, downs, _, sums, pairs_of = lax.fori_loop(
                0, length // STEP, step, (zero, zero, ones, zero, none), unroll=4
            )
            lags = lags or pairs_of
            low = bottom()
            for m in range(WAVE):
                top_half = jnp.where(low, swap_halves(downs[m]), ups[m])
                end_half = jnp.where(low, downs[m], swap_halves(ups[m]))
                piece = half * MODES + group + m
                keep[piece] = jnp.where(first, top_half, end_half)
                send[piece] = jnp.where(first, end_half, top_half)
                inner = lags[-1]
                for lag in reversed(range(STEP - 1)):
                    inner = decay[m] * inner + lags[lag]
                inner = inner + decay[m] * sums[m]
                within[piece : piece + 1, :] = jnp.sum(inner, axis=0, keepdims=True)


def near_kernel(work_u, work_g, residue, rate, near, back):
    length = near.shape[1] // 8
    for half in range(2):
        decay = [spread(jnp.exp(-rate[n : n + 1, lanes_of(half)])) for n in range(MODES)]
        weight = [spread(residue[n : n + 1, lanes_of(half)]) for n in range(MODES)]
        for source, target, reverse in ((work_u, near, False), (work_g, back, True)):

            def step(i, states, half=half, source=source, target=target, reverse=reverse, decay=decay, weight=weight):
                index = length - 1 - i if reverse else i
                rows = pl.ds(pl.multiple_of(index * 8, 8), 8)
                value = source[half, rows, :]
                states = tuple(decay[n] * states[n] + value for n in range(MODES))
                target[half, rows, :] = tree([weight[n] * states[n] for n in range(MODES)])
                return states

            lax.fori_loop(0, length, step, tuple(jnp.zeros((8, LANES), F32) for _ in range(MODES)), unroll=2)


def tree(parts):
    while len(parts) > 1:
        parts = [parts[i] + parts[i + 1] for i in range(0, len(parts), 2)]
    return parts[0]


def order(first, own, other):
    return jnp.where(first, own, other), jnp.where(first, other, own)


def pair_kernel(core, own, other, within, rate, out, *, block):
    first = core[0] == 0
    low = bottom()
    for half in range(2):
        for n in range(MODES):
            piece = half * MODES + n
            pace = rate[n : n + 1, lanes_of(half)]
            decay = spread(jnp.exp(-pace * float(block)))
            left, right = order(first, own[piece], other[piece])
            joined = jnp.where(low, left + decay * right, decay * left + right)
            cross = jnp.where(low, 0.0, left * swap_halves(right))
            total = jnp.exp(-pace) * jnp.sum(cross, axis=0, keepdims=True)
            for row in range(8):
                out[piece * ROWS + row] = joined[row : row + 1, :]
            out[piece * ROWS + 8] = within[piece : piece + 1, :] + total


def scan_kernel(pieces, pace, out, *, block):
    count = pieces.shape[0] // ROWS
    decay = jnp.exp(-pace[...] * float(block))
    decay4 = jnp.broadcast_to(decay, (4, LANES))

    def load(index, base):
        return jnp.concatenate([pieces[index * ROWS + base + j] for j in range(4)], axis=0)

    ahead = jnp.zeros((4, LANES), F32)
    cross = jnp.zeros((4, LANES), F32)
    local = jnp.zeros((1, LANES), F32)
    for index in range(count):
        for j in range(4):
            out[index * ROWS + j] = ahead[j : j + 1, :]
        cross = cross + ahead * load(index, 4)
        local = local + pieces[index * ROWS + 8]
        ahead = decay4 * ahead + load(index, 0)
    behind = jnp.zeros((4, LANES), F32)
    for index in reversed(range(count)):
        for j in range(4):
            out[index * ROWS + 4 + j] = behind[j : j + 1, :]
        behind = decay4 * behind + load(index, 4)
    total = local + jnp.exp(-pace[...]) * jnp.sum(cross, axis=0, keepdims=True)
    for index in range(count):
        out[index * ROWS + 8] = total


def split_kernel(core, pieces, own, other, rate, keep, send, total, share, sems, *, block):
    first = core[0] == 0
    low = bottom()
    for piece in range(2 * MODES):
        share[piece : piece + 1, :] = pieces[piece * ROWS + 8]
    copies = [pltpu.make_async_copy(share, total.at[i], sems.at[i]) for i in range(total.shape[0])]
    for copy in copies:
        copy.start()
    for half in range(2):
        for n in range(MODES):
            piece = half * MODES + n
            pace = rate[n : n + 1, lanes_of(half)]
            decay = spread(jnp.exp(-pace * float(block)))
            left, right = order(first, own[piece], other[piece])
            outer = jnp.concatenate([pieces[piece * ROWS + row] for row in range(8)], axis=0)
            inner = decay * outer + jnp.where(low, right, left)
            for_left = jnp.where(low, inner, outer)
            for_right = jnp.where(low, outer, inner)
            mine, others = order(first, for_left, for_right)
            keep[piece] = mine
            send[piece] = others
    for copy in copies:
        copy.wait()


def final_kernel(
    core,
    query_in,
    key_in,
    value_in,
    grad_in,
    residue,
    rate,
    near,
    back,
    own,
    other,
    mixed_out,
    grad_query_out,
    grad_key_out,
    grad_value_out,
    work,
    query,
    key,
    value,
    grad,
    mixed,
    grad_query,
    grad_key,
    grad_value,
    in_sems,
    sems,
):
    length = query.shape[1]
    repeat = query.shape[2] // (2 * LANES)
    first = core[0] == 0
    low = bottom()
    outs = ((mixed, mixed_out), (grad_query, grad_query_out), (grad_key, grad_key_out), (grad_value, grad_value_out))

    fore, aft = ((query_in, query), (grad_in, grad)), ((value_in, value), (key_in, key))
    for half in range(2):
        fetch(fore, in_sems, half, repeat, False)
        fetch(aft, in_sems, half, repeat, False, 2)

    def products(half, source_a, source_b, base):
        target_a, target_b = outs[base][0], outs[base + 1][0]
        for rep in range(repeat):
            cut = columns(half, rep)
            for seq in range(2):
                shared = work[pl.ds(seq * repeat + rep, length, stride=8), :]
                target_a[seq, :, cut] = (source_a[seq, :, cut].astype(F32) * shared).astype(jnp.bfloat16)
                target_b[seq, :, cut] = (source_b[seq, :, cut].astype(F32) * shared).astype(jnp.bfloat16)
            for which in (base, base + 1):
                slab_copy(*outs[which], sems, which, half, rep).start()

    for half in range(2):
        decay, forward, backward = [], [], []
        for n in range(MODES):
            piece = half * MODES + n
            weight = spread(residue[n : n + 1, lanes_of(half)])
            decay.append(spread(jnp.exp(-rate[n : n + 1, lanes_of(half)])))
            one, two = order(first, own[piece], other[piece])
            forward.append(weight * jnp.where(low, swap_halves(two), one))
            backward.append(weight * jnp.where(low, two, swap_halves(one)))

        def step(i, carry, decay=decay, half=half, source=near):
            carry = [decay[n] * carry[n] for n in range(MODES)]
            rows = pl.ds(pl.multiple_of(i * 8, 8), 8)
            work[rows, :] = source[half, rows, :] + tree(carry)
            return tuple(carry)

        def step_back(i, carry, step=step):
            return step(length - 1 - i, carry, source=back)

        lax.fori_loop(0, length, step, tuple(forward), unroll=2)
        fetch(fore, in_sems, half, repeat, True)
        products(half, query, grad, 0)
        lax.fori_loop(0, length, step_back, tuple(backward), unroll=2)
        fetch(aft, in_sems, half, repeat, True, 2)
        products(half, value, key, 2)
    for which in range(4):
        for half in range(2):
            for rep in range(repeat):
                slab_copy(*outs[which], sems, which, half, rep).wait()


VMEM = pl.BlockSpec(memory_space=pltpu.VMEM)
SMEM = pl.BlockSpec(memory_space=pltpu.SMEM)
HBM = pl.BlockSpec(memory_space=pltpu.HBM)


def room(mebibytes):
    return pltpu.CompilerParams(vmem_limit_bytes=int(mebibytes * 2**20))


def struct(*shape, dtype=F32):
    return jax.ShapeDtypeStruct(shape, dtype)


def staged(query, key, value, grad_out, residue, rate):
    seq_count, block, channels = query.shape
    pieces = 2 * MODES
    core = lax.axis_index("core").astype(jnp.int32).reshape(1)
    tile = struct(pieces, 8, LANES)
    rows = struct(pieces * ROWS, 1, LANES)
    works = struct(2, block * 8, LANES)
    whole = struct(*query.shape, dtype=jnp.bfloat16)
    repeat = channels // (2 * LANES)
    inputs = tuple(pltpu.with_memory_space_constraint(x, pltpu.HBM) for x in (query, key, value, grad_out))
    buffers = [pltpu.VMEM(query.shape, jnp.bfloat16)] * 4
    arrivals = [pltpu.SemaphoreType.DMA((4, 2, repeat))]
    work_u, work_g, keep, send, within = pl.pallas_call(
        sums_kernel,
        name="sums",
        out_shape=(works, works, tile, tile, struct(pieces, LANES)),
        in_specs=[SMEM] + [HBM] * 5,
        out_specs=(VMEM,) * 5,
        scratch_shapes=buffers + [pltpu.VMEM(rate.shape, F32)] + arrivals + [pltpu.SemaphoreType.DMA],
        compiler_params=room(12),
    )(core, *inputs, pltpu.with_memory_space_constraint(rate, pltpu.HBM))
    near, back = pl.pallas_call(
        near_kernel,
        name="near",
        out_shape=(works, works),
        in_specs=[VMEM] * 4,
        out_specs=(VMEM,) * 2,
        input_output_aliases={0: 0, 1: 1},
        compiler_params=room(12),
        cost_estimate=pl.CostEstimate(flops=2**26, transcendentals=0, bytes_accessed=2**22),
    )(work_u, work_g, residue, rate)
    exchange = [(0, 1), (1, 0)]
    other = lax.ppermute(send, "core", exchange)
    joined = pl.pallas_call(
        functools.partial(pair_kernel, block=block),
        name="pair",
        out_shape=rows,
        in_specs=[SMEM] + [VMEM] * 4,
        out_specs=VMEM,
        compiler_params=room(4),
    )(core, keep, other, within, rate)
    gathered = lax.all_to_all(joined, ("xh", "z"), 0, 0, tiled=True)
    gathered, near, back = lax.optimization_barrier((gathered, near, back))
    pace = lax.dynamic_slice(rate, (lax.axis_index("z"), lax.axis_index("xh") * LANES), (1, LANES))
    scanned = pl.pallas_call(
        functools.partial(scan_kernel, block=2 * block),
        name="scan",
        out_shape=pltpu.VMEM(rows.shape, F32),
        in_specs=[VMEM] * 2,
        out_specs=VMEM,
        compiler_params=room(4),
    )(gathered, pace)
    returned = lax.all_to_all(scanned, ("xh", "z"), 0, 0, tiled=True)
    group = lax.axis_size("core") * lax.axis_size("tensor")
    state, state_send, total = pl.pallas_call(
        functools.partial(split_kernel, block=block),
        name="split",
        out_shape=(tile, tile, struct(group, pieces, LANES)),
        in_specs=[SMEM] + [VMEM] * 4,
        out_specs=(VMEM, VMEM, HBM),
        scratch_shapes=[pltpu.VMEM((pieces, LANES), F32), pltpu.SemaphoreType.DMA((group,))],
        compiler_params=room(4),
    )(core, returned, keep, other, rate)
    state_other = lax.ppermute(state_send, "core", exchange)
    shares = lax.all_to_all(total, ("core", "tensor"), 0, 0, tiled=True)
    summed = jnp.sum(shares, axis=0)
    length = block * lax.axis_size(("xh", "z", "core"))
    summed = jnp.concatenate([summed[:MODES], summed[MODES:]], axis=1)
    grad_residue = summed / float(seq_count * length)
    mixed, grad_query, grad_key, grad_value = pl.pallas_call(
        final_kernel,
        name="final",
        out_shape=(whole,) * 4,
        in_specs=[SMEM] + [HBM] * 4 + [VMEM] * 6,
        out_specs=(HBM,) * 4,
        scratch_shapes=[pltpu.VMEM((block * 8, LANES), F32)] + buffers * 2 + arrivals * 2,
        compiler_params=room(12),
    )(core, *inputs, residue, rate, near, back, state, state_other)
    return (mixed, grad_query, grad_key, grad_value, grad_residue)


def solution(mesh):
    shape = (2, 16, 2, mesh.shape["tensor"])
    split = Mesh(mesh.devices.reshape(shape), ("xh", "z", "core", "tensor"))
    spec = P(None, ("xh", "z", "core"), "tensor")
    specs = (spec, spec, spec, spec)
    return jax.shard_map(staged, mesh=split, in_specs=specs + (P(), P()), out_specs=specs + (P(),), check_vma=False)
```

```python
import functools

import jax
import jax.numpy as jnp
from jax import lax
from jax.experimental import pallas as pl
from jax.experimental.pallas import tpu as pltpu
from jax.sharding import Mesh, PartitionSpec as P

F32 = jnp.float32
LANES = 128
MODES = 16
STEP = 4
WAVE = 4
ROWS = 9


def spread(row):
    return jnp.broadcast_to(row, (8, LANES))


def bottom():
    return lax.broadcasted_iota(jnp.int32, (8, LANES), 0) >= 4


def swap_halves(tile):
    return pltpu.roll(tile, 4, 0)


def lanes_of(half):
    return pl.ds(half * LANES, LANES)


def columns(half, rep):
    return pl.ds(rep * 2 * LANES + half * LANES, LANES)


def slab_copy(source, target, sems, which, half, rep):
    cut = columns(half, rep)
    return pltpu.make_async_copy(source.at[:, :, cut], target.at[:, :, cut], sems.at[which, half, rep])


def fetch(pairs, sems, half, repeat, wait, base=0):
    for rep in range(repeat):
        for which, (source, target) in enumerate(pairs):
            copy = slab_copy(source, target, sems, base + which, half, rep)
            copy.wait() if wait else copy.start()


def products_of(half, rep, first, second, work, repeat):
    length = first.shape[1]
    cut = columns(half, rep)
    for seq in range(2):
        rows = pl.ds(seq * repeat + rep, length, stride=8)
        work[half, rows, :] = first[seq, :, cut].astype(F32) * second[seq, :, cut].astype(F32)


def sums_kernel(
    core,
    query_in,
    key_in,
    value_in,
    grad_in,
    rate_in,
    work_u,
    work_g,
    keep,
    send,
    within,
    query,
    key,
    value,
    grad,
    rate,
    sems,
    rate_sem,
):
    length = query.shape[1]
    repeat = query.shape[2] // (2 * LANES)
    first = core[0] == 0
    pairs = ((key_in, key), (value_in, value), (grad_in, grad), (query_in, query))
    fetch(pairs, sems, 0, repeat, False)
    rates = pltpu.make_async_copy(rate_in, rate, rate_sem)
    rates.start()
    fetch(pairs, sems, 1, repeat, False)
    for half in range(2):
        if half == 0:
            rates.wait()
        batch = repeat if half else max(repeat // 2, 1)
        for start in range(0, repeat, batch):
            reps = range(start, start + batch)
            for rep in reps:
                for which, (source, target) in enumerate(pairs):
                    slab_copy(source, target, sems, which, half, rep).wait()
            for rep in reps:
                products_of(half, rep, key, value, work_u, repeat)
                products_of(half, rep, grad, query, work_g, repeat)
        lags = None
        for group in range(0, MODES, WAVE):
            modes = range(group, group + WAVE)
            decay = [spread(jnp.exp(-rate[n : n + 1, lanes_of(half)])) for n in modes]
            jump = [spread(jnp.exp(-rate[n : n + 1, lanes_of(half)] * float(STEP))) for n in modes]

            def step(i, carry, decay=decay, jump=jump, half=half):
                ups, downs, powers, sums, pairs = (list(c) for c in carry)
                base = i * (8 * STEP)
                rows = [pl.ds(pl.multiple_of(base + 8 * j, 8), 8) for j in range(STEP)]
                us = [work_u[half, row, :] for row in rows]
                gs = [work_g[half, row, :] for row in rows]
                for lag in range(len(pairs)):
                    for j in range(lag, STEP):
                        pairs[lag] = pairs[lag] + gs[j] * us[j - lag]
                for m in range(WAVE):
                    risen, fallen = us[0], gs[-1]
                    for j in range(1, STEP):
                        risen = decay[m] * risen + us[j]
                        fallen = decay[m] * fallen + gs[STEP - 1 - j]
                    sums[m] = sums[m] + fallen * ups[m]
                    ups[m] = jump[m] * ups[m] + risen
                    downs[m] = downs[m] + powers[m] * fallen
                    powers[m] = powers[m] * jump[m]
                return tuple(ups), tuple(downs), tuple(powers), tuple(sums), tuple(pairs)

            zero = tuple(jnp.zeros((8, LANES), F32) for _ in range(WAVE))
            ones = tuple(jnp.ones((8, LANES), F32) for _ in range(WAVE))
            none = () if lags else tuple(jnp.zeros((8, LANES), F32) for _ in range(STEP))
            ups, downs, _, sums, pairs_of = lax.fori_loop(
                0, length // STEP, step, (zero, zero, ones, zero, none), unroll=8
            )
            lags = lags or pairs_of
            low = bottom()
            for m in range(WAVE):
                top_half = jnp.where(low, swap_halves(downs[m]), ups[m])
                end_half = jnp.where(low, downs[m], swap_halves(ups[m]))
                piece = half * MODES + group + m
                keep[piece] = jnp.where(first, top_half, end_half)
                send[piece] = jnp.where(first, end_half, top_half)
                inner = lags[-1]
                for lag in reversed(range(STEP - 1)):
                    inner = decay[m] * inner + lags[lag]
                inner = inner + decay[m] * sums[m]
                within[piece : piece + 1, :] = jnp.sum(inner, axis=0, keepdims=True)


def near_kernel(work_u, work_g, residue, rate, near, back):
    length = near.shape[1] // 8
    for half in range(2):
        decay = [spread(jnp.exp(-rate[n : n + 1, lanes_of(half)])) for n in range(MODES)]
        weight = [spread(residue[n : n + 1, lanes_of(half)]) for n in range(MODES)]
        for source, target, reverse in ((work_u, near, False), (work_g, back, True)):

            def step(i, states, half=half, source=source, target=target, reverse=reverse, decay=decay, weight=weight):
                index = length - 1 - i if reverse else i
                rows = pl.ds(pl.multiple_of(index * 8, 8), 8)
                value = source[half, rows, :]
                states = tuple(decay[n] * states[n] + value for n in range(MODES))
                target[half, rows, :] = tree([weight[n] * states[n] for n in range(MODES)])
                return states

            lax.fori_loop(0, length, step, tuple(jnp.zeros((8, LANES), F32) for _ in range(MODES)), unroll=2)


def tree(parts):
    while len(parts) > 1:
        parts = [parts[i] + parts[i + 1] for i in range(0, len(parts), 2)]
    return parts[0]


def order(first, own, other):
    return jnp.where(first, own, other), jnp.where(first, other, own)


def pair_kernel(core, own, other, within, rate, out, *, block):
    first = core[0] == 0
    low = bottom()
    for half in range(2):
        for n in range(MODES):
            piece = half * MODES + n
            pace = rate[n : n + 1, lanes_of(half)]
            decay = spread(jnp.exp(-pace * float(block)))
            left, right = order(first, own[piece], other[piece])
            joined = jnp.where(low, left + decay * right, decay * left + right)
            cross = jnp.where(low, 0.0, left * swap_halves(right))
            total = jnp.exp(-pace) * jnp.sum(cross, axis=0, keepdims=True)
            for row in range(8):
                out[piece * ROWS + row] = joined[row : row + 1, :]
            out[piece * ROWS + 8] = within[piece : piece + 1, :] + total


def scan_kernel(pieces, pace, out, *, block):
    count = pieces.shape[0] // ROWS
    decay = jnp.exp(-pace[...] * float(block))
    decay4 = jnp.broadcast_to(decay, (4, LANES))

    def load(index, base):
        return jnp.concatenate([pieces[index * ROWS + base + j] for j in range(4)], axis=0)

    ahead = jnp.zeros((4, LANES), F32)
    cross = jnp.zeros((4, LANES), F32)
    local = jnp.zeros((1, LANES), F32)
    for index in range(count):
        for j in range(4):
            out[index * ROWS + j] = ahead[j : j + 1, :]
        cross = cross + ahead * load(index, 4)
        local = local + pieces[index * ROWS + 8]
        ahead = decay4 * ahead + load(index, 0)
    behind = jnp.zeros((4, LANES), F32)
    for index in reversed(range(count)):
        for j in range(4):
            out[index * ROWS + 4 + j] = behind[j : j + 1, :]
        behind = decay4 * behind + load(index, 4)
    total = local + jnp.exp(-pace[...]) * jnp.sum(cross, axis=0, keepdims=True)
    for index in range(count):
        out[index * ROWS + 8] = total


def split_kernel(core, pieces, own, other, rate, keep, send, total, share, sems, *, block):
    first = core[0] == 0
    low = bottom()
    for piece in range(2 * MODES):
        share[piece : piece + 1, :] = pieces[piece * ROWS + 8]
    copies = [pltpu.make_async_copy(share, total.at[i], sems.at[i]) for i in range(total.shape[0])]
    for copy in copies:
        copy.start()
    for half in range(2):
        for n in range(MODES):
            piece = half * MODES + n
            pace = rate[n : n + 1, lanes_of(half)]
            decay = spread(jnp.exp(-pace * float(block)))
            left, right = order(first, own[piece], other[piece])
            outer = jnp.concatenate([pieces[piece * ROWS + row] for row in range(8)], axis=0)
            inner = decay * outer + jnp.where(low, right, left)
            for_left = jnp.where(low, inner, outer)
            for_right = jnp.where(low, outer, inner)
            mine, others = order(first, for_left, for_right)
            keep[piece] = mine
            send[piece] = others
    for copy in copies:
        copy.wait()


def final_kernel(
    core,
    query_in,
    key_in,
    value_in,
    grad_in,
    residue,
    rate,
    near,
    back,
    own,
    other,
    mixed_out,
    grad_query_out,
    grad_key_out,
    grad_value_out,
    work,
    query,
    key,
    value,
    grad,
    mixed,
    grad_query,
    grad_key,
    grad_value,
    in_sems,
    sems,
):
    length = query.shape[1]
    repeat = query.shape[2] // (2 * LANES)
    first = core[0] == 0
    low = bottom()
    outs = ((mixed, mixed_out), (grad_query, grad_query_out), (grad_key, grad_key_out), (grad_value, grad_value_out))

    fore, aft = ((query_in, query), (grad_in, grad)), ((value_in, value), (key_in, key))
    for half in range(2):
        fetch(fore, in_sems, half, repeat, False)
        fetch(aft, in_sems, half, repeat, False, 2)

    def products(half, source_a, source_b, base):
        target_a, target_b = outs[base][0], outs[base + 1][0]
        for rep in range(repeat):
            cut = columns(half, rep)
            for seq in range(2):
                shared = work[pl.ds(seq * repeat + rep, length, stride=8), :]
                target_a[seq, :, cut] = (source_a[seq, :, cut].astype(F32) * shared).astype(jnp.bfloat16)
                target_b[seq, :, cut] = (source_b[seq, :, cut].astype(F32) * shared).astype(jnp.bfloat16)
            for which in (base, base + 1):
                slab_copy(*outs[which], sems, which, half, rep).start()

    for half in range(2):
        decay, forward, backward = [], [], []
        for n in range(MODES):
            piece = half * MODES + n
            weight = spread(residue[n : n + 1, lanes_of(half)])
            decay.append(spread(jnp.exp(-rate[n : n + 1, lanes_of(half)])))
            one, two = order(first, own[piece], other[piece])
            forward.append(weight * jnp.where(low, swap_halves(two), one))
            backward.append(weight * jnp.where(low, two, swap_halves(one)))

        def step(i, carry, decay=decay, half=half, source=near):
            carry = [decay[n] * carry[n] for n in range(MODES)]
            rows = pl.ds(pl.multiple_of(i * 8, 8), 8)
            work[rows, :] = source[half, rows, :] + tree(carry)
            return tuple(carry)

        def step_back(i, carry, step=step):
            return step(length - 1 - i, carry, source=back)

        lax.fori_loop(0, length, step, tuple(forward), unroll=4)
        fetch(fore, in_sems, half, repeat, True)
        products(half, query, grad, 0)
        lax.fori_loop(0, length, step_back, tuple(backward), unroll=4)
        fetch(aft, in_sems, half, repeat, True, 2)
        products(half, value, key, 2)
    for which in range(4):
        for half in range(2):
            for rep in range(repeat):
                slab_copy(*outs[which], sems, which, half, rep).wait()


VMEM = pl.BlockSpec(memory_space=pltpu.VMEM)
SMEM = pl.BlockSpec(memory_space=pltpu.SMEM)
HBM = pl.BlockSpec(memory_space=pltpu.HBM)


def room(mebibytes):
    return pltpu.CompilerParams(vmem_limit_bytes=int(mebibytes * 2**20))


def struct(*shape, dtype=F32):
    return jax.ShapeDtypeStruct(shape, dtype)


def staged(query, key, value, grad_out, residue, rate):
    seq_count, block, channels = query.shape
    pieces = 2 * MODES
    core = lax.axis_index("core").astype(jnp.int32).reshape(1)
    tile = struct(pieces, 8, LANES)
    rows = struct(pieces * ROWS, 1, LANES)
    works = struct(2, block * 8, LANES)
    whole = struct(*query.shape, dtype=jnp.bfloat16)
    repeat = channels // (2 * LANES)
    inputs = tuple(pltpu.with_memory_space_constraint(x, pltpu.HBM) for x in (query, key, value, grad_out))
    buffers = [pltpu.VMEM(query.shape, jnp.bfloat16)] * 4
    arrivals = [pltpu.SemaphoreType.DMA((4, 2, repeat))]
    work_u, work_g, keep, send, within = pl.pallas_call(
        sums_kernel,
        name="sums",
        out_shape=(works, works, tile, tile, struct(pieces, LANES)),
        in_specs=[SMEM] + [HBM] * 5,
        out_specs=(VMEM,) * 5,
        scratch_shapes=buffers + [pltpu.VMEM(rate.shape, F32)] + arrivals + [pltpu.SemaphoreType.DMA],
        compiler_params=room(12),
    )(core, *inputs, pltpu.with_memory_space_constraint(rate, pltpu.HBM))
    near, back = pl.pallas_call(
        near_kernel,
        name="near",
        out_shape=(works, works),
        in_specs=[VMEM] * 4,
        out_specs=(VMEM,) * 2,
        input_output_aliases={0: 0, 1: 1},
        compiler_params=room(12),
        cost_estimate=pl.CostEstimate(flops=2**26, transcendentals=0, bytes_accessed=2**22),
    )(work_u, work_g, residue, rate)
    exchange = [(0, 1), (1, 0)]
    other = lax.ppermute(send, "core", exchange)
    joined = pl.pallas_call(
        functools.partial(pair_kernel, block=block),
        name="pair",
        out_shape=rows,
        in_specs=[SMEM] + [VMEM] * 4,
        out_specs=VMEM,
        compiler_params=room(4),
    )(core, keep, other, within, rate)
    gathered = lax.all_to_all(joined, ("xh", "z"), 0, 0, tiled=True)
    gathered, near, back = lax.optimization_barrier((gathered, near, back))
    pace = lax.dynamic_slice(rate, (lax.axis_index("z"), lax.axis_index("xh") * LANES), (1, LANES))
    scanned = pl.pallas_call(
        functools.partial(scan_kernel, block=2 * block),
        name="scan",
        out_shape=pltpu.VMEM(rows.shape, F32),
        in_specs=[VMEM] * 2,
        out_specs=VMEM,
        compiler_params=room(4),
    )(gathered, pace)
    returned = lax.all_to_all(scanned, ("xh", "z"), 0, 0, tiled=True)
    group = lax.axis_size("core") * lax.axis_size("tensor")
    state, state_send, total = pl.pallas_call(
        functools.partial(split_kernel, block=block),
        name="split",
        out_shape=(tile, tile, struct(group, pieces, LANES)),
        in_specs=[SMEM] + [VMEM] * 4,
        out_specs=(VMEM, VMEM, HBM),
        scratch_shapes=[pltpu.VMEM((pieces, LANES), F32), pltpu.SemaphoreType.DMA((group,))],
        compiler_params=room(4),
    )(core, returned, keep, other, rate)
    state_other = lax.ppermute(state_send, "core", exchange)
    shares = lax.all_to_all(total, ("core", "tensor"), 0, 0, tiled=True)
    summed = jnp.sum(shares, axis=0)
    length = block * lax.axis_size(("xh", "z", "core"))
    summed = jnp.concatenate([summed[:MODES], summed[MODES:]], axis=1)
    grad_residue = summed / float(seq_count * length)
    mixed, grad_query, grad_key, grad_value = pl.pallas_call(
        final_kernel,
        name="final",
        out_shape=(whole,) * 4,
        in_specs=[SMEM] + [HBM] * 4 + [VMEM] * 6,
        out_specs=(HBM,) * 4,
        scratch_shapes=[pltpu.VMEM((block * 8, LANES), F32)] + buffers * 2 + arrivals * 2,
        compiler_params=room(12),
    )(core, *inputs, residue, rate, near, back, state, state_other)
    return (mixed, grad_query, grad_key, grad_value, grad_residue)


def solution(mesh):
    shape = (2, 16, 2, mesh.shape["tensor"])
    split = Mesh(mesh.devices.reshape(shape), ("xh", "z", "core", "tensor"))
    spec = P(None, ("xh", "z", "core"), "tensor")
    specs = (spec, spec, spec, spec)
    return jax.shard_map(staged, mesh=split, in_specs=specs + (P(), P()), out_specs=specs + (P(),), check_vma=False)
```

```python
import functools

import jax
import jax.numpy as jnp
from jax import lax
from jax.experimental import pallas as pl
from jax.experimental.pallas import tpu as pltpu
from jax.sharding import Mesh, PartitionSpec as P

F32 = jnp.float32
LANES = 128
MODES = 16
STEP = 4
WAVE = 4
ROWS = 9


def spread(row):
    return jnp.broadcast_to(row, (8, LANES))


def lanes_of(half):
    return pl.ds(half * LANES, LANES)


def columns(half, rep):
    return pl.ds(rep * 2 * LANES + half * LANES, LANES)


def slab_copy(source, target, sems, which, half, rep):
    cut = columns(half, rep)
    return pltpu.make_async_copy(source.at[:, :, cut], target.at[:, :, cut], sems.at[which, half, rep])


def fetch(pairs, sems, half, repeat, wait, base=0):
    for rep in range(repeat):
        for which, (source, target) in enumerate(pairs):
            copy = slab_copy(source, target, sems, base + which, half, rep)
            copy.wait() if wait else copy.start()


def products_of(half, rep, first, second, work, repeat):
    length = first.shape[1]
    cut = columns(half, rep)
    for seq in range(2):
        rows = pl.ds(seq * repeat + rep, length, stride=8)
        work[half, rows, :] = first[seq, :, cut].astype(F32) * second[seq, :, cut].astype(F32)


def sums_kernel(
    core,
    query_in,
    key_in,
    value_in,
    grad_in,
    rate_in,
    work_u,
    work_g,
    keep,
    send,
    query,
    key,
    value,
    grad,
    rate,
    raw_u,
    raw_g,
    shares,
    sems,
    rate_sem,
):
    length = query.shape[1]
    repeat = query.shape[2] // (2 * LANES)
    first = core[0] == 0
    pairs = ((key_in, key), (value_in, value), (grad_in, grad), (query_in, query))
    fetch(pairs, sems, 0, repeat, False)
    rates = pltpu.make_async_copy(rate_in, rate, rate_sem)
    rates.start()
    fetch(pairs, sems, 1, repeat, False)
    for half in range(2):
        if half == 0:
            rates.wait()
        batch = repeat if half else max(repeat // 2, 1)
        for start in range(0, repeat, batch):
            reps = range(start, start + batch)
            for rep in reps:
                for which, (source, target) in enumerate(pairs):
                    slab_copy(source, target, sems, which, half, rep).wait()
            for rep in reps:
                products_of(half, rep, key, value, work_u, repeat)
                products_of(half, rep, grad, query, work_g, repeat)
        lags = None
        for group in range(0, MODES, WAVE):
            modes = range(group, group + WAVE)
            decay = [spread(jnp.exp(-rate[n : n + 1, lanes_of(half)])) for n in modes]
            jump = [spread(jnp.exp(-rate[n : n + 1, lanes_of(half)] * float(STEP))) for n in modes]

            def step(i, carry, decay=decay, jump=jump, half=half):
                ups, downs, powers, sums, pairs = (list(c) for c in carry)
                base = i * (8 * STEP)
                rows = [pl.ds(pl.multiple_of(base + 8 * j, 8), 8) for j in range(STEP)]
                us = [work_u[half, row, :] for row in rows]
                gs = [work_g[half, row, :] for row in rows]
                for lag in range(len(pairs)):
                    for j in range(lag, STEP):
                        pairs[lag] = pairs[lag] + gs[j] * us[j - lag]
                for m in range(WAVE):
                    risen, fallen = us[0], gs[-1]
                    for j in range(1, STEP):
                        risen = decay[m] * risen + us[j]
                        fallen = decay[m] * fallen + gs[STEP - 1 - j]
                    sums[m] = sums[m] + fallen * ups[m]
                    ups[m] = jump[m] * ups[m] + risen
                    downs[m] = downs[m] + powers[m] * fallen
                    powers[m] = powers[m] * jump[m]
                return tuple(ups), tuple(downs), tuple(powers), tuple(sums), tuple(pairs)

            zero = tuple(jnp.zeros((8, LANES), F32) for _ in range(WAVE))
            ones = tuple(jnp.ones((8, LANES), F32) for _ in range(WAVE))
            none = () if lags else tuple(jnp.zeros((8, LANES), F32) for _ in range(STEP))
            ups, downs, _, sums, pairs_of = lax.fori_loop(
                0, length // STEP, step, (zero, zero, ones, zero, none), unroll=8
            )
            lags = lags or pairs_of
            for m in range(WAVE):
                piece = half * MODES + group + m
                raw_u[piece] = ups[m]
                raw_g[piece] = downs[m]
                inner = lags[-1]
                for lag in reversed(range(STEP - 1)):
                    inner = decay[m] * inner + lags[lag]
                inner = inner + decay[m] * sums[m]
                shares[piece : piece + 1, :] = jnp.sum(inner, axis=0, keepdims=True)
        for m in range(MODES // 2):
            one, two = half * MODES + m, half * MODES + MODES // 2 + m
            spot = half * (MODES // 2) + m
            for which, raw in enumerate((raw_u, raw_g)):
                keep[2 * spot + which] = jnp.where(first, raw[one], raw[two])
                send[2 * spot + which] = jnp.where(first, raw[two], raw[one])
        one = shares[half * MODES : half * MODES + MODES // 2, :]
        two = shares[half * MODES + MODES // 2 : (half + 1) * MODES, :]
        keep[2 * MODES + half] = jnp.where(first, one, two)
        send[2 * MODES + half] = jnp.where(first, two, one)


def near_kernel(work_u, work_g, residue, rate, near, back):
    length = near.shape[1] // 8
    for half in range(2):
        decay = [spread(jnp.exp(-rate[n : n + 1, lanes_of(half)])) for n in range(MODES)]
        weight = [spread(residue[n : n + 1, lanes_of(half)]) for n in range(MODES)]
        for source, target, reverse in ((work_u, near, False), (work_g, back, True)):

            def step(i, states, half=half, source=source, target=target, reverse=reverse, decay=decay, weight=weight):
                index = length - 1 - i if reverse else i
                rows = pl.ds(pl.multiple_of(index * 8, 8), 8)
                value = source[half, rows, :]
                states = tuple(decay[n] * states[n] + value for n in range(MODES))
                target[half, rows, :] = tree([weight[n] * states[n] for n in range(MODES)])
                return states

            lax.fori_loop(0, length, step, tuple(jnp.zeros((8, LANES), F32) for _ in range(MODES)), unroll=2)


def tree(parts):
    while len(parts) > 1:
        parts = [parts[i] + parts[i + 1] for i in range(0, len(parts), 2)]
    return parts[0]


def order(first, own, other):
    return jnp.where(first, own, other), jnp.where(first, other, own)


def own_rate(first, rate, m, half):
    one = rate[m : m + 1, lanes_of(half)]
    two = rate[MODES // 2 + m : MODES // 2 + m + 1, lanes_of(half)]
    return jnp.where(first, one, two)


def pair_kernel(core, own, other, rate, out, *, block):
    first = core[0] == 0
    for half in range(2):
        within = own[2 * MODES + half] + other[2 * MODES + half]
        for m in range(MODES // 2):
            spot = half * (MODES // 2) + m
            pace = own_rate(first, rate, m, half)
            decay = spread(jnp.exp(-pace * float(block)))
            left_u, right_u = order(first, own[2 * spot], other[2 * spot])
            left_g, right_g = order(first, own[2 * spot + 1], other[2 * spot + 1])
            rising = decay * left_u + right_u
            falling = left_g + decay * right_g
            cross = jnp.exp(-pace) * jnp.sum(left_u * right_g, axis=0, keepdims=True)
            for seq in range(2):
                start = (2 * spot + seq) * ROWS
                for j in range(4):
                    out[start + j] = rising[4 * seq + j : 4 * seq + j + 1, :]
                    out[start + 4 + j] = falling[4 * seq + j : 4 * seq + j + 1, :]
            out[2 * spot * ROWS + 8] = within[m : m + 1, :] + cross
            out[(2 * spot + 1) * ROWS + 8] = jnp.zeros((1, LANES), F32)


def scan_kernel(pieces, pace, out, *, block):
    count = pieces.shape[0] // ROWS
    decay = jnp.exp(-pace[...] * float(block))
    decay4 = jnp.broadcast_to(decay, (4, LANES))

    def load(index, base):
        return jnp.concatenate([pieces[index * ROWS + base + j] for j in range(4)], axis=0)

    ahead = jnp.zeros((4, LANES), F32)
    cross = jnp.zeros((4, LANES), F32)
    local = jnp.zeros((1, LANES), F32)
    for index in range(count):
        for j in range(4):
            out[index * ROWS + j] = ahead[j : j + 1, :]
        cross = cross + ahead * load(index, 4)
        local = local + pieces[index * ROWS + 8]
        ahead = decay4 * ahead + load(index, 0)
    behind = jnp.zeros((4, LANES), F32)
    for index in reversed(range(count)):
        for j in range(4):
            out[index * ROWS + 4 + j] = behind[j : j + 1, :]
        behind = decay4 * behind + load(index, 4)
    total = local + jnp.exp(-pace[...]) * jnp.sum(cross, axis=0, keepdims=True)
    for index in range(count):
        out[index * ROWS + 8] = total


def split_kernel(core, pieces, own, other, rate, keep, send, total, share, sems, *, block):
    first = core[0] == 0
    for spot in range(MODES):
        share[spot : spot + 1, :] = pieces[2 * spot * ROWS + 8] + pieces[(2 * spot + 1) * ROWS + 8]
    copies = [pltpu.make_async_copy(share, total.at[i], sems.at[i]) for i in range(total.shape[0])]
    for copy in copies:
        copy.start()
    for half in range(2):
        for m in range(MODES // 2):
            spot = half * (MODES // 2) + m
            decay = spread(jnp.exp(-own_rate(first, rate, m, half) * float(block)))
            left_u, _ = order(first, own[2 * spot], other[2 * spot])
            _, right_g = order(first, own[2 * spot + 1], other[2 * spot + 1])
            rows = [[pieces[(2 * spot + seq) * ROWS + base + j] for seq in range(2) for j in range(4)] for base in (0, 4)]
            ahead, behind = (jnp.concatenate(r, axis=0) for r in rows)
            ahead_right = decay * ahead + left_u
            behind_left = decay * behind + right_g
            keep[2 * spot] = jnp.where(first, ahead, ahead_right)
            send[2 * spot] = jnp.where(first, ahead_right, ahead)
            keep[2 * spot + 1] = jnp.where(first, behind_left, behind)
            send[2 * spot + 1] = jnp.where(first, behind, behind_left)
    for copy in copies:
        copy.wait()


def final_kernel(
    core,
    query_in,
    key_in,
    value_in,
    grad_in,
    residue,
    rate,
    near,
    back,
    own,
    other,
    mixed_out,
    grad_query_out,
    grad_key_out,
    grad_value_out,
    work,
    query,
    key,
    value,
    grad,
    mixed,
    grad_query,
    grad_key,
    grad_value,
    in_sems,
    sems,
):
    length = query.shape[1]
    repeat = query.shape[2] // (2 * LANES)
    first = core[0] == 0
    outs = ((mixed, mixed_out), (grad_query, grad_query_out), (grad_key, grad_key_out), (grad_value, grad_value_out))

    fore, aft = ((query_in, query), (grad_in, grad)), ((value_in, value), (key_in, key))
    for half in range(2):
        fetch(fore, in_sems, half, repeat, False)
        fetch(aft, in_sems, half, repeat, False, 2)

    def products(half, source_a, source_b, base):
        target_a, target_b = outs[base][0], outs[base + 1][0]
        for rep in range(repeat):
            cut = columns(half, rep)
            for seq in range(2):
                shared = work[pl.ds(seq * repeat + rep, length, stride=8), :]
                target_a[seq, :, cut] = (source_a[seq, :, cut].astype(F32) * shared).astype(jnp.bfloat16)
                target_b[seq, :, cut] = (source_b[seq, :, cut].astype(F32) * shared).astype(jnp.bfloat16)
            for which in (base, base + 1):
                slab_copy(*outs[which], sems, which, half, rep).start()

    for half in range(2):
        decay, forward, backward = [], [], []
        for n in range(MODES):
            spot = half * (MODES // 2) + n % (MODES // 2)
            weight = spread(residue[n : n + 1, lanes_of(half)])
            decay.append(spread(jnp.exp(-rate[n : n + 1, lanes_of(half)])))
            mine = first if n < MODES // 2 else jnp.logical_not(first)
            forward.append(weight * jnp.where(mine, own[2 * spot], other[2 * spot]))
            backward.append(weight * jnp.where(mine, own[2 * spot + 1], other[2 * spot + 1]))

        def step(i, carry, decay=decay, half=half, source=near):
            carry = [decay[n] * carry[n] for n in range(MODES)]
            rows = pl.ds(pl.multiple_of(i * 8, 8), 8)
            work[rows, :] = source[half, rows, :] + tree(carry)
            return tuple(carry)

        def step_back(i, carry, step=step):
            return step(length - 1 - i, carry, source=back)

        lax.fori_loop(0, length, step, tuple(forward), unroll=4)
        fetch(fore, in_sems, half, repeat, True)
        products(half, query, grad, 0)
        lax.fori_loop(0, length, step_back, tuple(backward), unroll=4)
        fetch(aft, in_sems, half, repeat, True, 2)
        products(half, value, key, 2)
    for which in range(4):
        for half in range(2):
            for rep in range(repeat):
                slab_copy(*outs[which], sems, which, half, rep).wait()


VMEM = pl.BlockSpec(memory_space=pltpu.VMEM)
SMEM = pl.BlockSpec(memory_space=pltpu.SMEM)
HBM = pl.BlockSpec(memory_space=pltpu.HBM)


def room(mebibytes):
    return pltpu.CompilerParams(vmem_limit_bytes=int(mebibytes * 2**20))


def struct(*shape, dtype=F32):
    return jax.ShapeDtypeStruct(shape, dtype)


def staged(query, key, value, grad_out, residue, rate):
    seq_count, block, channels = query.shape
    pieces = 2 * MODES
    core = lax.axis_index("core").astype(jnp.int32).reshape(1)
    tile = struct(pieces, 8, LANES)
    swaps = struct(pieces + 2, 8, LANES)
    rows = struct(pieces * ROWS, 1, LANES)
    works = struct(2, block * 8, LANES)
    whole = struct(*query.shape, dtype=jnp.bfloat16)
    repeat = channels // (2 * LANES)
    inputs = tuple(pltpu.with_memory_space_constraint(x, pltpu.HBM) for x in (query, key, value, grad_out))
    buffers = [pltpu.VMEM(query.shape, jnp.bfloat16)] * 4
    arrivals = [pltpu.SemaphoreType.DMA((4, 2, repeat))]
    work_u, work_g, keep, send = pl.pallas_call(
        sums_kernel,
        name="sums",
        out_shape=(works, works, swaps, swaps),
        in_specs=[SMEM] + [HBM] * 5,
        out_specs=(VMEM,) * 4,
        scratch_shapes=buffers
        + [pltpu.VMEM(rate.shape, F32)]
        + [pltpu.VMEM(tile.shape, F32)] * 2
        + [pltpu.VMEM((pieces, LANES), F32)]
        + arrivals
        + [pltpu.SemaphoreType.DMA],
        compiler_params=room(12),
    )(core, *inputs, pltpu.with_memory_space_constraint(rate, pltpu.HBM))
    near, back = pl.pallas_call(
        near_kernel,
        name="near",
        out_shape=(works, works),
        in_specs=[VMEM] * 4,
        out_specs=(VMEM,) * 2,
        input_output_aliases={0: 0, 1: 1},
        compiler_params=room(12),
        cost_estimate=pl.CostEstimate(flops=2**26, transcendentals=0, bytes_accessed=2**22),
    )(work_u, work_g, residue, rate)
    exchange = [(0, 1), (1, 0)]
    other = lax.ppermute(send, "core", exchange)
    joined = pl.pallas_call(
        functools.partial(pair_kernel, block=block),
        name="pair",
        out_shape=rows,
        in_specs=[SMEM] + [VMEM] * 3,
        out_specs=VMEM,
        compiler_params=room(4),
    )(core, keep, other, rate)
    gathered = lax.all_to_all(joined, ("xh", "z"), 0, 0, tiled=True)
    gathered, near, back = lax.optimization_barrier((gathered, near, back))
    mode = lax.axis_index("core") * (MODES // 2) + lax.axis_index("z") // 2
    pace = lax.dynamic_slice(rate, (mode, lax.axis_index("xh") * LANES), (1, LANES))
    scanned = pl.pallas_call(
        functools.partial(scan_kernel, block=2 * block),
        name="scan",
        out_shape=pltpu.VMEM(rows.shape, F32),
        in_specs=[VMEM] * 2,
        out_specs=VMEM,
        compiler_params=room(4),
    )(gathered, pace)
    returned = lax.all_to_all(scanned, ("xh", "z"), 0, 0, tiled=True)
    group = lax.axis_size("core") * lax.axis_size("tensor")
    state, state_send, total = pl.pallas_call(
        functools.partial(split_kernel, block=block),
        name="split",
        out_shape=(tile, tile, struct(group, MODES, LANES)),
        in_specs=[SMEM] + [VMEM] * 4,
        out_specs=(VMEM, VMEM, HBM),
        scratch_shapes=[pltpu.VMEM((MODES, LANES), F32), pltpu.SemaphoreType.DMA((group,))],
        compiler_params=room(4),
    )(core, returned, keep, other, rate)
    state_other = lax.ppermute(state_send, "core", exchange)
    shares = lax.all_to_all(total, ("core", "tensor"), 0, 0, tiled=True)
    summed = jnp.sum(shares.reshape(2, group // 2, MODES, LANES), axis=1).reshape(2, 2, MODES // 2, LANES)
    summed = jnp.concatenate([summed[:, 0].reshape(MODES, LANES), summed[:, 1].reshape(MODES, LANES)], axis=1)
    length = block * lax.axis_size(("xh", "z", "core"))
    grad_residue = summed / float(seq_count * length)
    mixed, grad_query, grad_key, grad_value = pl.pallas_call(
        final_kernel,
        name="final",
        out_shape=(whole,) * 4,
        in_specs=[SMEM] + [HBM] * 4 + [VMEM] * 6,
        out_specs=(HBM,) * 4,
        scratch_shapes=[pltpu.VMEM((block * 8, LANES), F32)] + buffers * 2 + arrivals * 2,
        compiler_params=room(12),
    )(core, *inputs, residue, rate, near, back, state, state_other)
    return (mixed, grad_query, grad_key, grad_value, grad_residue)


def solution(mesh):
    shape = (2, 16, 2, mesh.shape["tensor"])
    split = Mesh(mesh.devices.reshape(shape), ("xh", "z", "core", "tensor"))
    spec = P(None, ("xh", "z", "core"), "tensor")
    specs = (spec, spec, spec, spec)
    return jax.shard_map(staged, mesh=split, in_specs=specs + (P(), P()), out_specs=specs + (P(),), check_vma=False)
```

```python
import functools

import jax
import jax.numpy as jnp
from jax import lax
from jax.experimental import pallas as pl
from jax.experimental.pallas import tpu as pltpu
from jax.sharding import Mesh, PartitionSpec as P

F32 = jnp.float32
LANES = 128
MODES = 16
STEP = 4
WAVE = 4
ROWS = 9


def spread(row):
    return jnp.broadcast_to(row, (8, LANES))


def lanes_of(half):
    return pl.ds(half * LANES, LANES)


def columns(half, rep):
    return pl.ds(rep * 2 * LANES + half * LANES, LANES)


def slab_copy(source, target, sems, which, half, rep):
    cut = columns(half, rep)
    return pltpu.make_async_copy(source.at[:, :, cut], target.at[:, :, cut], sems.at[which, half, rep])


def fetch(pairs, sems, half, repeat, wait, base=0):
    for rep in range(repeat):
        for which, (source, target) in enumerate(pairs):
            copy = slab_copy(source, target, sems, base + which, half, rep)
            copy.wait() if wait else copy.start()


def products_of(half, rep, first, second, work, repeat):
    length = first.shape[1]
    cut = columns(half, rep)
    for seq in range(2):
        rows = pl.ds(seq * repeat + rep, length, stride=8)
        work[half, rows, :] = first[seq, :, cut].astype(F32) * second[seq, :, cut].astype(F32)


def sums_kernel(
    core,
    query_in,
    key_in,
    value_in,
    grad_in,
    rate_in,
    work_u,
    work_g,
    keep,
    send,
    query,
    key,
    value,
    grad,
    rate,
    raw_u,
    raw_g,
    shares,
    sems,
    rate_sem,
):
    length = query.shape[1]
    repeat = query.shape[2] // (2 * LANES)
    first = core[0] == 0
    pairs = ((key_in, key), (value_in, value), (grad_in, grad), (query_in, query))
    fetch(pairs, sems, 0, repeat, False)
    rates = pltpu.make_async_copy(rate_in, rate, rate_sem)
    rates.start()
    fetch(pairs, sems, 1, repeat, False)
    for half in range(2):
        if half == 0:
            rates.wait()
        batch = repeat if half else max(repeat // 2, 1)
        for start in range(0, repeat, batch):
            reps = range(start, start + batch)
            for rep in reps:
                for which, (source, target) in enumerate(pairs):
                    slab_copy(source, target, sems, which, half, rep).wait()
            for rep in reps:
                products_of(half, rep, key, value, work_u, repeat)
                products_of(half, rep, grad, query, work_g, repeat)
        lags = None
        for group in range(0, MODES, WAVE):
            modes = range(group, group + WAVE)
            decay = [spread(jnp.exp(-rate[n : n + 1, lanes_of(half)])) for n in modes]
            jump = [spread(jnp.exp(-rate[n : n + 1, lanes_of(half)] * float(STEP))) for n in modes]

            def step(i, carry, decay=decay, jump=jump, half=half):
                ups, downs, powers, sums, pairs = (list(c) for c in carry)
                base = i * (8 * STEP)
                rows = [pl.ds(pl.multiple_of(base + 8 * j, 8), 8) for j in range(STEP)]
                us = [work_u[half, row, :] for row in rows]
                gs = [work_g[half, row, :] for row in rows]
                for lag in range(len(pairs)):
                    for j in range(lag, STEP):
                        pairs[lag] = pairs[lag] + gs[j] * us[j - lag]
                for m in range(WAVE):
                    risen, fallen = us[0], gs[-1]
                    for j in range(1, STEP):
                        risen = decay[m] * risen + us[j]
                        fallen = decay[m] * fallen + gs[STEP - 1 - j]
                    sums[m] = sums[m] + fallen * ups[m]
                    ups[m] = jump[m] * ups[m] + risen
                    downs[m] = downs[m] + powers[m] * fallen
                    powers[m] = powers[m] * jump[m]
                return tuple(ups), tuple(downs), tuple(powers), tuple(sums), tuple(pairs)

            zero = tuple(jnp.zeros((8, LANES), F32) for _ in range(WAVE))
            ones = tuple(jnp.ones((8, LANES), F32) for _ in range(WAVE))
            none = () if lags else tuple(jnp.zeros((8, LANES), F32) for _ in range(STEP))
            ups, downs, _, sums, pairs_of = lax.fori_loop(
                0, length // STEP, step, (zero, zero, ones, zero, none), unroll=8
            )
            lags = lags or pairs_of
            for m in range(WAVE):
                piece = half * MODES + group + m
                raw_u[piece] = ups[m]
                raw_g[piece] = downs[m]
                inner = lags[-1]
                for lag in reversed(range(STEP - 1)):
                    inner = decay[m] * inner + lags[lag]
                inner = inner + decay[m] * sums[m]
                shares[piece : piece + 1, :] = jnp.sum(inner, axis=0, keepdims=True)
        for m in range(MODES // 2):
            one, two = half * MODES + m, half * MODES + MODES // 2 + m
            spot = half * (MODES // 2) + m
            for which, raw in enumerate((raw_u, raw_g)):
                keep[2 * spot + which] = jnp.where(first, raw[one], raw[two])
                send[2 * spot + which] = jnp.where(first, raw[two], raw[one])
        one = shares[half * MODES : half * MODES + MODES // 2, :]
        two = shares[half * MODES + MODES // 2 : (half + 1) * MODES, :]
        keep[2 * MODES + half] = jnp.where(first, one, two)
        send[2 * MODES + half] = jnp.where(first, two, one)


def near_kernel(work_u, work_g, residue, rate, near, back):
    length = near.shape[1] // 8
    for half in range(2):
        decay = [spread(jnp.exp(-rate[n : n + 1, lanes_of(half)])) for n in range(MODES)]
        weight = [spread(residue[n : n + 1, lanes_of(half)]) for n in range(MODES)]
        for source, target, reverse in ((work_u, near, False), (work_g, back, True)):

            def step(i, states, half=half, source=source, target=target, reverse=reverse, decay=decay, weight=weight):
                index = length - 1 - i if reverse else i
                rows = pl.ds(pl.multiple_of(index * 8, 8), 8)
                value = source[half, rows, :]
                states = tuple(decay[n] * states[n] + value for n in range(MODES))
                target[half, rows, :] = tree([weight[n] * states[n] for n in range(MODES)])
                return states

            lax.fori_loop(0, length, step, tuple(jnp.zeros((8, LANES), F32) for _ in range(MODES)), unroll=2)


def tree(parts):
    while len(parts) > 1:
        parts = [parts[i] + parts[i + 1] for i in range(0, len(parts), 2)]
    return parts[0]


def order(first, own, other):
    return jnp.where(first, own, other), jnp.where(first, other, own)


def own_rate(first, rate, m, half):
    one = rate[m : m + 1, lanes_of(half)]
    two = rate[MODES // 2 + m : MODES // 2 + m + 1, lanes_of(half)]
    return jnp.where(first, one, two)


def pair_kernel(core, own, other, rate, out, *, block):
    first = core[0] == 0
    for half in range(2):
        within = own[2 * MODES + half] + other[2 * MODES + half]
        for m in range(MODES // 2):
            spot = half * (MODES // 2) + m
            pace = own_rate(first, rate, m, half)
            decay = spread(jnp.exp(-pace * float(block)))
            left_u, right_u = order(first, own[2 * spot], other[2 * spot])
            left_g, right_g = order(first, own[2 * spot + 1], other[2 * spot + 1])
            rising = decay * left_u + right_u
            falling = left_g + decay * right_g
            cross = jnp.exp(-pace) * jnp.sum(left_u * right_g, axis=0, keepdims=True)
            for seq in range(2):
                start = (2 * spot + seq) * ROWS
                for j in range(4):
                    out[start + j] = rising[4 * seq + j : 4 * seq + j + 1, :]
                    out[start + 4 + j] = falling[4 * seq + j : 4 * seq + j + 1, :]
            out[2 * spot * ROWS + 8] = within[m : m + 1, :] + cross
            out[(2 * spot + 1) * ROWS + 8] = jnp.zeros((1, LANES), F32)


def scan_kernel(pieces, pace, out, *, block):
    count = pieces.shape[0] // ROWS
    decay = jnp.exp(-pace[...] * float(block))
    decay4 = jnp.broadcast_to(decay, (4, LANES))

    def load(index, base):
        return jnp.concatenate([pieces[index * ROWS + base + j] for j in range(4)], axis=0)

    ahead = jnp.zeros((4, LANES), F32)
    cross = jnp.zeros((4, LANES), F32)
    local = jnp.zeros((1, LANES), F32)
    for index in range(count):
        for j in range(4):
            out[index * ROWS + j] = ahead[j : j + 1, :]
        cross = cross + ahead * load(index, 4)
        local = local + pieces[index * ROWS + 8]
        ahead = decay4 * ahead + load(index, 0)
    behind = jnp.zeros((4, LANES), F32)
    for index in reversed(range(count)):
        for j in range(4):
            out[index * ROWS + 4 + j] = behind[j : j + 1, :]
        behind = decay4 * behind + load(index, 4)
    total = local + jnp.exp(-pace[...]) * jnp.sum(cross, axis=0, keepdims=True)
    for index in range(count):
        out[index * ROWS + 8] = total


def split_kernel(core, pieces, own, other, rate, keep, send, total, share, sems, *, block):
    first = core[0] == 0
    for spot in range(MODES):
        share[spot : spot + 1, :] = pieces[2 * spot * ROWS + 8] + pieces[(2 * spot + 1) * ROWS + 8]
    copies = [pltpu.make_async_copy(share, total.at[i], sems.at[i]) for i in range(total.shape[0])]
    for copy in copies:
        copy.start()
    for half in range(2):
        for m in range(MODES // 2):
            spot = half * (MODES // 2) + m
            decay = spread(jnp.exp(-own_rate(first, rate, m, half) * float(block)))
            left_u, _ = order(first, own[2 * spot], other[2 * spot])
            _, right_g = order(first, own[2 * spot + 1], other[2 * spot + 1])
            rows = [[pieces[(2 * spot + seq) * ROWS + base + j] for seq in range(2) for j in range(4)] for base in (0, 4)]
            ahead, behind = (jnp.concatenate(r, axis=0) for r in rows)
            ahead_right = decay * ahead + left_u
            behind_left = decay * behind + right_g
            keep[2 * spot] = jnp.where(first, ahead, ahead_right)
            send[2 * spot] = jnp.where(first, ahead_right, ahead)
            keep[2 * spot + 1] = jnp.where(first, behind_left, behind)
            send[2 * spot + 1] = jnp.where(first, behind, behind_left)
    for copy in copies:
        copy.wait()


def final_kernel(
    core,
    query,
    key_in,
    value_in,
    grad_in,
    residue,
    rate,
    near,
    back,
    own,
    other,
    mixed_out,
    grad_query_out,
    grad_key_out,
    grad_value_out,
    work,
    key,
    value,
    grad,
    mixed,
    grad_query,
    grad_key,
    grad_value,
    in_sems,
    sems,
):
    length = query.shape[1]
    repeat = query.shape[2] // (2 * LANES)
    first = core[0] == 0
    outs = ((mixed, mixed_out), (grad_query, grad_query_out), (grad_key, grad_key_out), (grad_value, grad_value_out))

    fore, aft = ((grad_in, grad),), ((value_in, value), (key_in, key))
    for half in range(2):
        fetch(fore, in_sems, half, repeat, False)
        fetch(aft, in_sems, half, repeat, False, 2)

    def products(half, source_a, source_b, base):
        target_a, target_b = outs[base][0], outs[base + 1][0]
        for rep in range(repeat):
            cut = columns(half, rep)
            for seq in range(2):
                shared = work[pl.ds(seq * repeat + rep, length, stride=8), :]
                target_a[seq, :, cut] = (source_a[seq, :, cut].astype(F32) * shared).astype(jnp.bfloat16)
                target_b[seq, :, cut] = (source_b[seq, :, cut].astype(F32) * shared).astype(jnp.bfloat16)
            for which in (base, base + 1):
                slab_copy(*outs[which], sems, which, half, rep).start()

    for half in range(2):
        decay, forward, backward = [], [], []
        for n in range(MODES):
            spot = half * (MODES // 2) + n % (MODES // 2)
            weight = spread(residue[n : n + 1, lanes_of(half)])
            decay.append(spread(jnp.exp(-rate[n : n + 1, lanes_of(half)])))
            mine = first if n < MODES // 2 else jnp.logical_not(first)
            forward.append(weight * jnp.where(mine, own[2 * spot], other[2 * spot]))
            backward.append(weight * jnp.where(mine, own[2 * spot + 1], other[2 * spot + 1]))

        def step(i, carry, decay=decay, half=half, source=near):
            carry = [decay[n] * carry[n] for n in range(MODES)]
            rows = pl.ds(pl.multiple_of(i * 8, 8), 8)
            work[rows, :] = source[half, rows, :] + tree(carry)
            return tuple(carry)

        def step_back(i, carry, step=step):
            return step(length - 1 - i, carry, source=back)

        lax.fori_loop(0, length, step, tuple(forward), unroll=4)
        fetch(fore, in_sems, half, repeat, True)
        products(half, query, grad, 0)
        lax.fori_loop(0, length, step_back, tuple(backward), unroll=4)
        fetch(aft, in_sems, half, repeat, True, 2)
        products(half, value, key, 2)
    for which in range(4):
        for half in range(2):
            for rep in range(repeat):
                slab_copy(*outs[which], sems, which, half, rep).wait()


VMEM = pl.BlockSpec(memory_space=pltpu.VMEM)
SMEM = pl.BlockSpec(memory_space=pltpu.SMEM)
HBM = pl.BlockSpec(memory_space=pltpu.HBM)


def room(mebibytes):
    return pltpu.CompilerParams(vmem_limit_bytes=int(mebibytes * 2**20))


def struct(*shape, dtype=F32):
    return jax.ShapeDtypeStruct(shape, dtype)


def staged(query, key, value, grad_out, residue, rate):
    seq_count, block, channels = query.shape
    pieces = 2 * MODES
    core = lax.axis_index("core").astype(jnp.int32).reshape(1)
    tile = struct(pieces, 8, LANES)
    swaps = struct(pieces + 2, 8, LANES)
    rows = struct(pieces * ROWS, 1, LANES)
    works = struct(2, block * 8, LANES)
    whole = struct(*query.shape, dtype=jnp.bfloat16)
    repeat = channels // (2 * LANES)
    inputs = tuple(pltpu.with_memory_space_constraint(x, pltpu.HBM) for x in (query, key, value, grad_out))
    buffers = [pltpu.VMEM(query.shape, jnp.bfloat16)] * 4
    arrivals = [pltpu.SemaphoreType.DMA((4, 2, repeat))]
    work_u, work_g, keep, send = pl.pallas_call(
        sums_kernel,
        name="sums",
        out_shape=(works, works, swaps, swaps),
        in_specs=[SMEM] + [HBM] * 5,
        out_specs=(VMEM,) * 4,
        scratch_shapes=buffers
        + [pltpu.VMEM(rate.shape, F32)]
        + [pltpu.VMEM(tile.shape, F32)] * 2
        + [pltpu.VMEM((pieces, LANES), F32)]
        + arrivals
        + [pltpu.SemaphoreType.DMA],
        compiler_params=room(12),
    )(core, *inputs, pltpu.with_memory_space_constraint(rate, pltpu.HBM))
    near, back = pl.pallas_call(
        near_kernel,
        name="near",
        out_shape=(works, works),
        in_specs=[VMEM] * 4,
        out_specs=(VMEM,) * 2,
        input_output_aliases={0: 0, 1: 1},
        compiler_params=room(12),
        cost_estimate=pl.CostEstimate(flops=2**26, transcendentals=0, bytes_accessed=2**22),
    )(work_u, work_g, residue, rate)
    exchange = [(0, 1), (1, 0)]
    other = lax.ppermute(send, "core", exchange)
    joined = pl.pallas_call(
        functools.partial(pair_kernel, block=block),
        name="pair",
        out_shape=rows,
        in_specs=[SMEM] + [VMEM] * 3,
        out_specs=VMEM,
        compiler_params=room(4),
    )(core, keep, other, rate)
    gathered = lax.all_to_all(joined, ("xh", "z"), 0, 0, tiled=True)
    gathered, near, back = lax.optimization_barrier((gathered, near, back))
    mode = lax.axis_index("core") * (MODES // 2) + lax.axis_index("z") // 2
    pace = lax.dynamic_slice(rate, (mode, lax.axis_index("xh") * LANES), (1, LANES))
    scanned = pl.pallas_call(
        functools.partial(scan_kernel, block=2 * block),
        name="scan",
        out_shape=pltpu.VMEM(rows.shape, F32),
        in_specs=[VMEM] * 2,
        out_specs=VMEM,
        compiler_params=room(4),
    )(gathered, pace)
    returned = lax.all_to_all(scanned, ("xh", "z"), 0, 0, tiled=True)
    group = lax.axis_size("core") * lax.axis_size("tensor")
    state, state_send, total = pl.pallas_call(
        functools.partial(split_kernel, block=block),
        name="split",
        out_shape=(tile, tile, struct(group, MODES, LANES)),
        in_specs=[SMEM] + [VMEM] * 4,
        out_specs=(VMEM, VMEM, HBM),
        scratch_shapes=[pltpu.VMEM((MODES, LANES), F32), pltpu.SemaphoreType.DMA((group,))],
        compiler_params=room(4),
    )(core, returned, keep, other, rate)
    state_other = lax.ppermute(state_send, "core", exchange)
    shares = lax.all_to_all(total, ("core", "tensor"), 0, 0, tiled=True)
    summed = jnp.sum(shares.reshape(2, group // 2, MODES, LANES), axis=1).reshape(2, 2, MODES // 2, LANES)
    summed = jnp.concatenate([summed[:, 0].reshape(MODES, LANES), summed[:, 1].reshape(MODES, LANES)], axis=1)
    length = block * lax.axis_size(("xh", "z", "core"))
    grad_residue = summed / float(seq_count * length)
    mixed, grad_query, grad_key, grad_value = pl.pallas_call(
        final_kernel,
        name="final",
        out_shape=(whole,) * 4,
        in_specs=[SMEM] + [VMEM] + [HBM] * 3 + [VMEM] * 6,
        out_specs=(HBM,) * 4,
        scratch_shapes=[pltpu.VMEM((block * 8, LANES), F32)] + buffers[:3] + buffers + arrivals * 2,
        compiler_params=room(12),
    )(core, query, *inputs[1:], residue, rate, near, back, state, state_other)
    return (mixed, grad_query, grad_key, grad_value, grad_residue)


def solution(mesh):
    shape = (2, 16, 2, mesh.shape["tensor"])
    split = Mesh(mesh.devices.reshape(shape), ("xh", "z", "core", "tensor"))
    spec = P(None, ("xh", "z", "core"), "tensor")
    specs = (spec, spec, spec, spec)
    return jax.shard_map(staged, mesh=split, in_specs=specs + (P(), P()), out_specs=specs + (P(),), check_vma=False)
```
